32 devices in a mesh: orb: 2 (over x), grid: 16 (over z, y, core).
Axes of the slice: x: 2, y: 2, z: 4, core: 2. Of those that a mesh axis runs over, the one named last changes fastest.
Arguments:
- orbitals: bfloat16 [2, 1024, 2304], P('orb', 'grid'), may hold values from -6 to 6
- continuum: bfloat16 [4, 1024, 2304], P(None, 'grid'), may hold values from -6 to 6
- harmonic_table: bfloat16 [2560, 2304], P('orb'), may hold values from -0.125 to 0.125
- ang_weight: float32 [2560], P('orb'), may hold values from 0.5 to 2
- channel_lm: int32 [2304], replicated, may hold values from 0 to 2303, each once
Outputs:
- exchange_out: float32 [2304, 4, 1024], P('orb', None, 'grid')
The draws below stay inside these ranges and needn't reach their ends.
Inputs may be any that keep to these rules, and one draw needn't show every extreme that they name: channel_lm names each harmonic index lm = l * l + l + m (l up to 47) exactly once.
All inputs are finite; a program needn't handle non-finite values.
Results may differ from the reference program's by a relative error of at most 0.03.
Values may be sent and summed in bfloat16 or wider, within the bound.
No kernel may reach another device: no remote copies, remote signals or barrier semaphores. Data moves between devices by JAX's collectives and lax.ppermute only.
A program may use at most 128 MiB of HBM per device.

```python
import math
import jax
import jax.numpy as jnp
from jax import lax

LMAX = 47
LM = 2304
R = 1024
NANG = 2560
NC = 4
NORB = 2
N_ORB = 2


def steps_of(stream_key, extent, cuts, smallest, high):
    level, own = 1.0, jax.random.fold_in(stream_key, 6)
    for axis_at, shards_of in cuts:
        heights = jnp.exp(jax.random.uniform(jax.random.fold_in(own, axis_at), (shards_of,), jnp.float32, smallest / len(cuts), high / len(cuts)))
        level = level * jnp.repeat(heights, extent[axis_at] // shards_of).reshape([-1 if axis == axis_at else 1 for axis in range(len(extent))])
    return level


def noise(key, dims, spread, limit, pieces=(), kind=jnp.bfloat16):
    drawn = jax.random.normal(key, dims, jnp.float32) * spread
    if len(pieces) > 0:
        drawn = steps_of(key, dims, pieces, -0.22, 0.18) * drawn
    return jnp.clip(drawn, min=-limit, max=limit).astype(kind)


def setup_inputs(seed: int = 0) -> dict:
    keys = jax.random.split(jax.random.key(seed), 6)
    return {
        "orbitals": noise(keys[0], (NORB, R, LM), 1.0, 6.0, ((0, 2), (1, 16))),
        "continuum": noise(keys[1], (NC, R, LM), 1.0, 6.0, ((1, 16),)),
        "harmonic_table": noise(keys[2], (NANG, LM), LM ** -0.5, 0.125, ((0, 2),)),
        "ang_weight": jnp.clip(jnp.exp(math.log(2.0) - 1.3862944 * jax.random.uniform(keys[3], (NANG,), jnp.float32) ** steps_of(keys[3], (NANG,), ((0, 2),), -0.2, 0.2)), 0.5, 2.0),
        "channel_lm": jax.random.permutation(keys[4], LM).astype(jnp.int32),
    }


LOG_SPAN = 7.0


def radial_grid(points):
    logarithm_increment = LOG_SPAN / points
    positions = jnp.arange(points, dtype=jnp.float32)
    radius = jnp.exp((positions + 1.0 - points) * logarithm_increment)
    return logarithm_increment, radius, logarithm_increment * radius


def combine(earlier, later):
    return (earlier[0] * later[0], earlier[1] * later[0] + later[1])


def channel_degree(lm_index):
    levels = jnp.arange(1, LMAX + 1, dtype=jnp.int32)
    return jnp.sum((lm_index[:, None] >= levels * levels).astype(jnp.float32), axis=1)


def solve_poisson(density, degree):
    points = density.shape[-1]
    final_dimension = density.ndim - 1
    logarithm_increment, radius, weight = radial_grid(points)
    decay_rate = jnp.exp(-degree * logarithm_increment)[:, None, None]
    decays = jnp.broadcast_to(decay_rate, density.shape)
    source = weight * density
    inner_sum = lax.associative_scan(combine, (decays, source), axis=final_dimension)[1]
    outer_sum = lax.associative_scan(combine, (decays, source / radius), reverse=True, axis=final_dimension)[1]
    beyond = jnp.concatenate([outer_sum[..., 1:], jnp.zeros_like(outer_sum[..., :1])], axis=-1) * decay_rate
    factor = (4.0 / (2.0 * degree + 1.0))[:, None, None]
    return factor * (inner_sum / radius + beyond)


def reference(orbitals, continuum, harmonic_table, ang_weight, channel_lm):
    orbitals = jnp.transpose(orbitals, (0, 2, 1))
    continuum = jnp.transpose(continuum, (0, 2, 1))
    analysis = (ang_weight[:, None] * harmonic_table.astype(jnp.float32)).astype(jnp.bfloat16)
    continuum_angular = jnp.einsum('qd,wdm->qwm', harmonic_table.astype(jnp.float32), continuum.astype(jnp.float32)).astype(jnp.bfloat16)
    slices = NANG // N_ORB
    table_blocks = analysis.reshape(N_ORB, slices, LM)

    def angular_orbital(orbital):
        return jnp.dot(harmonic_table, orbital, preferred_element_type=jnp.float32).astype(jnp.bfloat16)

    def density_of(orbital):
        phi_ang = angular_orbital(orbital)
        pair_values = (phi_ang.astype(jnp.float32)[:, None, :] * continuum_angular.astype(jnp.float32)).astype(jnp.bfloat16)
        pair_blocks = pair_values.reshape(N_ORB, slices, NC * R)

        def add_block(running, items):
            table_block, value_block = items
            part_sum = jnp.dot(table_block.T, value_block, preferred_element_type=jnp.float32)
            rounded = lax.optimization_barrier(part_sum.astype(jnp.bfloat16))
            return running + rounded.astype(jnp.float32), None

        total, _ = lax.scan(add_block, jnp.zeros((LM, NC * R), jnp.float32), (table_blocks, pair_blocks))
        return total.astype(jnp.bfloat16).reshape(LM, NC, R)

    density = lax.map(density_of, orbitals)
    degree = channel_degree(channel_lm)

    def potential_of(one_density):
        return solve_poisson(one_density.astype(jnp.float32), degree).astype(jnp.bfloat16)

    potential = lax.map(potential_of, density)

    def collect(running, items):
        orbital, orbital_pot = items
        phi_ang = angular_orbital(orbital)
        pot_ang = jnp.dot(harmonic_table, orbital_pot.reshape(LM, NC * R), preferred_element_type=jnp.float32).reshape(NANG, NC, R)
        return running + phi_ang.astype(jnp.float32)[:, None, :] * pot_ang, None

    weighted_values, _ = lax.scan(collect, jnp.zeros((NANG, NC, R), jnp.float32), (orbitals, potential))
    product = weighted_values.astype(jnp.bfloat16)
    result = jnp.dot(analysis.T, product.reshape(NANG, NC * R), preferred_element_type=jnp.float32)
    return -result.reshape(LM, NC, R)
```

```python
import functools
import math

import jax
import jax.numpy as jnp
from jax import lax
from jax.experimental import pallas as pl
from jax.experimental.pallas import tpu as pltpu
from jax.sharding import PartitionSpec as P

LMAX = 47
LM = 2304


LOG_SPAN = 7.0


def combine(earlier, later):
    return (earlier[0] * later[0], earlier[1] * later[0] + later[1])


def channel_degree(lm_index):
    levels = jnp.arange(1, LMAX + 1, dtype=jnp.int32)
    return jnp.sum((lm_index[:, None] >= levels * levels).astype(jnp.float32), axis=1)


def line_sums(forward_source, backward_source, decay_rate, block_size):
    lead_first, lead_second, count, channels = forward_source.shape
    block_count = count // block_size
    forward_blocks = forward_source.reshape(
        lead_first, lead_second, block_count, block_size, channels
    )
    backward_blocks = backward_source.reshape(
        lead_first, lead_second, block_count, block_size, channels
    )
    forward = forward_blocks
    backward = backward_blocks
    for distance in range(1, block_size):
        factor = jnp.exp(-decay_rate * distance)
        padding = jnp.zeros((lead_first, lead_second, block_count, distance, channels), jnp.float32)
        forward = forward + factor * jnp.concatenate(
            [padding, forward_blocks[:, :, :, : block_size - distance]], axis=3
        )
        backward = backward + factor * jnp.concatenate(
            [backward_blocks[:, :, :, distance:], padding], axis=3
        )
    block_decay = jnp.broadcast_to(
        jnp.exp(-decay_rate * block_size), (lead_first, lead_second, block_count, channels)
    )
    forward_total = lax.associative_scan(
        combine, (block_decay, forward[:, :, :, block_size - 1]), axis=2
    )[1]
    backward_total = lax.associative_scan(
        combine, (block_decay, backward[:, :, :, 0]), reverse=True, axis=2
    )[1]
    boundary = jnp.zeros((lead_first, lead_second, 1, channels), jnp.float32)
    earlier_sum = jnp.concatenate([boundary, forward_total[:, :, : block_count - 1]], axis=2)
    later_sum = jnp.concatenate([backward_total[:, :, 1:], boundary], axis=2)
    offsets = jnp.arange(block_size, dtype=jnp.float32)[:, None]
    forward = forward + jnp.exp(-decay_rate * (offsets + 1.0)) * earlier_sum[:, :, :, None, :]
    backward = (
        backward + jnp.exp(-decay_rate * (block_size - offsets)) * later_sum[:, :, :, None, :]
    )
    shape = forward_source.shape
    return (
        forward.reshape(shape),
        backward.reshape(shape),
        forward_total[:, :, block_count - 1],
        backward_total[:, :, 0],
    )


def local_lines(density, degree, points):
    count = density.shape[2]
    increment = LOG_SPAN / points
    positions = jnp.arange(count, dtype=jnp.int32).astype(jnp.float32)[:, None]
    radius = jnp.exp((positions + 1.0 - points) * increment)
    decay_rate = degree * increment
    source = increment * radius * density
    scaled = increment * density
    forward, backward, forward_end, backward_end = line_sums(
        source, scaled, decay_rate, math.gcd(count, 16)
    )
    return (forward, backward, forward_end, backward_end, radius, scaled, decay_rate)


def finish_potential(forward, backward, radius, scaled, degree):
    factor = 4.0 / (2.0 * degree + 1.0)
    return factor * (forward / radius + backward - scaled)


def shards(orbitals, continuum, harmonic_table, ang_weight, channel_lm):
    analysis = (ang_weight[:, None] * harmonic_table.astype(jnp.float32)).astype(jnp.bfloat16)
    phi_ang = jnp.einsum(
        "al,irl->ira",
        harmonic_table,
        lax.all_gather(orbitals, "orb", axis=0, tiled=True),
        preferred_element_type=jnp.float32,
    ).astype(jnp.bfloat16)
    continuum_angular = jnp.einsum(
        "al,krl->kra", harmonic_table, continuum, preferred_element_type=jnp.float32
    ).astype(jnp.bfloat16)
    pair_values = (
        phi_ang.astype(jnp.float32)[:, None] * continuum_angular.astype(jnp.float32)[None]
    ).astype(jnp.bfloat16)
    density = lax.psum_scatter(
        jnp.einsum(
            "al,ikra->ikrl", analysis, pair_values, preferred_element_type=jnp.float32
        ).astype(jnp.bfloat16),
        "orb",
        scatter_dimension=0,
        tiled=True,
    )
    local_count = LM // lax.axis_size("grid")
    local_channel_index = lax.dynamic_slice_in_dim(
        channel_lm, lax.axis_index("grid") * local_count, local_count
    )
    degree = channel_degree(local_channel_index)
    line_density = lax.all_to_all(density, "grid", split_axis=3, concat_axis=2, tiled=True)
    points = line_density.shape[2]
    forward, backward, forward_end, backward_end, radius, scaled, decay_rate = local_lines(
        line_density.astype(jnp.float32), degree, points
    )
    potential = finish_potential(forward, backward, radius, scaled, degree).astype(jnp.bfloat16)
    radial_potential = lax.all_to_all(potential, "grid", split_axis=2, concat_axis=3, tiled=True)
    pot_ang = jnp.einsum(
        "al,ikrl->ikra",
        harmonic_table,
        lax.all_gather(radial_potential, "orb", axis=0, tiled=True),
        preferred_element_type=jnp.float32,
    )
    weighted_values = jnp.sum(phi_ang.astype(jnp.float32)[:, None] * pot_ang, axis=0)
    product = weighted_values.astype(jnp.bfloat16)
    return -lax.psum_scatter(
        jnp.einsum("al,kra->lkr", analysis, product, preferred_element_type=jnp.float32),
        "orb",
        scatter_dimension=0,
        tiled=True,
    )


NC = 4
NI = 2
NP = NI * NC
CHUNK = 256
TILE = 768
F32 = jnp.float32
BF16 = jnp.bfloat16


def dot_nt(a, b):
    return lax.dot_general(a, b, (((1,), (1,)), ((), ())), preferred_element_type=F32)


def dot_nn(a, b):
    return jnp.dot(a, b, preferred_element_type=F32)


def span_of(index, size):
    return pl.ds(pl.multiple_of(index * size, size), size)


def store_pairs(values, weight, points, pairs, span):
    phi = values[: NI * points].astype(F32) * weight
    psi = values[NI * points :].astype(F32)
    for i in range(NI):
        for k in range(NC):
            product = phi[i * points : (i + 1) * points] * psi[k * points : (k + 1) * points]
            row = (i * NC + k) * points
            pairs[row : row + points, span] = product.astype(BF16)


def own_kernel(
    step, place, own, other, cont, weight, degree_ref, table_hbm,
    part_ref, phi_ref, ends_ref,
    table, rows, pairs, work, sems,
):
    x = place[0]
    points = own.shape[0]
    half = points // 2
    steps = table.shape[0] // CHUNK

    def fetch(i):
        return pltpu.make_async_copy(
            table_hbm.at[span_of(i, CHUNK)], table.at[span_of(i, CHUNK)], sems.at[i]
        )

    for i in range(steps):
        fetch(i).start()
    rows[span_of(x, points), :] = own[...]
    rows[span_of(1 - x, points), :] = other[...]
    rows[NI * points :, :] = cont[...]

    def angular(i, carry):
        fetch(i).wait()
        span = span_of(i, CHUNK)
        values = dot_nt(rows[...], table[span, :]).astype(BF16)
        store_pairs(values, weight[:, span], points, pairs, span)
        for o in range(NI):
            lower = values[o * points : o * points + half]
            upper = values[o * points + half : (o + 1) * points]
            phi_ref[o * half : (o + 1) * half, span] = jnp.where(x == 0, lower, upper)
        return carry

    lax.fori_loop(0, steps, angular, 0)

    def density(t, carry):
        span = span_of(t, TILE)
        degree = degree_ref[:, span]
        work[...] = dot_nn(pairs[...], table[:, span])
        position = lax.broadcasted_iota(jnp.int32, (half, TILE), 0).astype(F32)
        ahead = jnp.exp((degree + 1.0) * step * (position - (half - 1.0)))
        behind = jnp.exp(-degree * step * position)
        for p in range(NP):
            low = work[p * points : p * points + half, :]
            high = work[p * points + half : (p + 1) * points, :]
            part_ref[p * half : (p + 1) * half, span] = jnp.where(x == 0, low, high).astype(BF16)
            ends = (low * ahead, high * ahead, low * behind, high * behind)
            for n in range(4):
                ends_ref[n * NP + p : n * NP + p + 1, span] = jnp.sum(ends[n], axis=0, keepdims=True)
        return carry

    lax.fori_loop(0, table.shape[1] // TILE, density, 0)


def finish_kernel(
    step, pieces, place, own, other, cont, weight, far_weight, degree_ref, earlier, later, part, phi, *refs
):
    table_hbm, far_hbm = refs[0], refs[1 : 1 + pieces]
    send_ref, keep_ref, table, rows, pairs, far_phi, pot, product, work, total, sems = refs[1 + pieces :]
    x = place[0]
    points = own.shape[0]
    half = points // 2
    quad = table_hbm.shape[0]
    size = quad // pieces
    steps = quad // CHUNK
    channels = table.shape[1]

    def fetch_far(n):
        start = pl.multiple_of(quad + place[1 + n], size)
        return pltpu.make_async_copy(far_hbm[n], table.at[pl.ds(start, size)], sems.at[n])

    fetch_own = pltpu.make_async_copy(table_hbm, table.at[pl.ds(0, quad)], sems.at[pieces])
    for n in range(pieces):
        fetch_far(n).start()
    fetch_own.start()
    rows[span_of(x, half), :] = own[span_of(x, half), :]
    rows[span_of(1 - x, half), :] = other[span_of(x, half), :]
    for k in range(NC):
        rows[(NI + k) * half : (NI + k + 1) * half, :] = cont[span_of(2 * k + x, half), :]
    for n in range(pieces):
        fetch_far(n).wait()

    def angular(i, carry):
        span = span_of(i, CHUNK)
        values = dot_nt(rows[...], table[span_of(i + steps, CHUNK), :]).astype(BF16)
        store_pairs(values, far_weight[:, span], half, pairs, span)
        far_phi[:, span] = values[: NI * half]
        return carry

    lax.fori_loop(0, steps, angular, 0)

    def radial(t, carry):
        span = span_of(t, TILE)
        degree = degree_ref[:, span]
        shrink_ahead = jnp.exp(-(degree + 1.0) * step)
        shrink_behind = jnp.exp(-degree * step)
        factor = 4.0 * step / (2.0 * degree + 1.0)
        far = dot_nn(pairs[...], table[quad:, span])
        density = part[:, span].astype(F32) + far.astype(BF16).astype(F32)
        density = density.astype(BF16).astype(F32)
        work[...] = density.reshape(NP, half, TILE)
        ahead = earlier[:, span]
        behind = later[:, span] * shrink_behind
        for j in range(half):
            ahead = ahead * shrink_ahead + work[:, j, :]
            total[:, j, :] = ahead
        for j in range(half - 1, -1, -1):
            total[:, j, :] = factor * (total[:, j, :] + behind)
            behind = (behind + work[:, j, :]) * shrink_behind
        pot[:, span] = total[...].reshape(NP * half, TILE).astype(BF16)
        return carry

    lax.fori_loop(0, channels // TILE, radial, 0)
    fetch_own.wait()

    def weigh(i, table_at, phi_at, weight_at, span):
        angle = dot_nt(pot[...], table[table_at, :])
        for k in range(NC):
            value = jnp.zeros((half, CHUNK), F32)
            for o in range(NI):
                value += phi_at[o * half : (o + 1) * half, span].astype(F32) * angle[
                    (o * NC + k) * half : (o * NC + k + 1) * half
                ]
            product[k * half : (k + 1) * half, table_at] = (value * weight_at[:, span]).astype(BF16)

    def near(i, carry):
        weigh(i, span_of(i, CHUNK), phi, weight, span_of(i, CHUNK))
        return carry

    def distant(i, carry):
        weigh(i, span_of(i + steps, CHUNK), far_phi, far_weight, span_of(i, CHUNK))
        return carry

    lax.fori_loop(0, steps, near, 0)
    lax.fori_loop(0, steps, distant, 0)
    share = channels // 2
    third = share // 3
    for t in range(3):
        away = pl.ds(pl.multiple_of((1 - x) * share + t * third, third), third)
        home = pl.ds(pl.multiple_of(x * share + t * third, third), third)
        columns = slice(t * third, (t + 1) * third)
        send_ref[:, columns] = (-dot_nn(product[...], table[:, away])).astype(BF16)
        keep_ref[:, columns] = -dot_nn(product[...], table[:, home])


def place_kernel(place, keep, came, out_ref):
    x = place[0]
    half = keep.shape[0] // NC
    mine = keep[...]
    theirs = came[...].astype(F32)
    lower = jnp.where(x == 0, mine, theirs)
    upper = jnp.where(x == 0, theirs, mine)
    for k in range(NC):
        rows = slice(k * half, (k + 1) * half)
        out_ref[:, k, :] = jnp.concatenate([lower[rows], upper[rows]], axis=0).T


VMEM_SPEC = pl.BlockSpec(memory_space=pltpu.VMEM)
SMEM_SPEC = pl.BlockSpec(memory_space=pltpu.SMEM)
HBM_SPEC = pl.BlockSpec(memory_space=pl.ANY)


def shards_by_table(orbitals, continuum, harmonic_table, ang_weight, channel_lm):
    quad, channels = harmonic_table.shape
    points = orbitals.shape[1]
    half = points // 2
    step = LOG_SPAN / (points * lax.axis_size("grid"))
    x = lax.axis_index("orb")
    g = lax.axis_index("grid")
    core, y, z = g % 2, (g // 2) % 2, g // 4
    across = [(0, 1), (1, 0)]
    everyone = range(16)

    def over_x(value):
        return lax.ppermute(value, "orb", across)

    def flip(value, bits):
        return lax.ppermute(value, "grid", [(n, n ^ bits) for n in everyone])

    pieces = 8
    size = quad // pieces
    corner = 2 * (z % 2) + y

    def offset(which, side):
        return (which * 2 + side) * size

    def slab(which):
        return lax.dynamic_slice_in_dim(harmonic_table, offset(which, core), size)

    own = orbitals[0]
    other = over_x(own)
    weight = ang_weight[None, :]
    far_weight = over_x(weight)
    first = over_x(slab(corner))
    last = over_x(slab(corner ^ 3))
    by_y = flip(first, 2)
    by_z = flip(first, 4)
    received = [first, last, by_y, by_z]
    which = [corner, corner ^ 3, corner ^ 1, corner ^ 2]
    far = received + [flip(value, 1) for value in received]
    offsets = [offset(w, core) for w in which] + [offset(w, 1 - core) for w in which]
    place = jnp.stack([x] + offsets).astype(jnp.int32)

    degree = channel_degree(channel_lm)[None, :]
    cont = continuum.reshape(NC * points, channels)
    part, phi, ends = pl.pallas_call(
        functools.partial(own_kernel, step),
        out_shape=(
            jax.ShapeDtypeStruct((NP * half, channels), BF16),
            jax.ShapeDtypeStruct((NI * half, quad), BF16),
            jax.ShapeDtypeStruct((4 * NP, channels), F32),
        ),
        in_specs=[SMEM_SPEC] + [VMEM_SPEC] * 5 + [HBM_SPEC],
        out_specs=(VMEM_SPEC,) * 3,
        scratch_shapes=[
            pltpu.VMEM((quad, channels), BF16),
            pltpu.VMEM(((NI + NC) * points, channels), BF16),
            pltpu.VMEM((NP * points, quad), BF16),
            pltpu.VMEM((NP * points, TILE), F32),
            pltpu.SemaphoreType.DMA((quad // CHUNK,)),
        ],
        compiler_params=pltpu.CompilerParams(vmem_limit_bytes=40 << 20),
        name="own_half",
    )(place, own, other, cont, weight, degree, harmonic_table)

    ends = (ends + over_x(ends.astype(BF16)).astype(F32)).reshape(4, NP, channels)
    ahead_rate = (degree + 1.0) * step
    behind_rate = degree * step

    def ahead_by(count):
        return jnp.exp(-ahead_rate * count)

    def behind_by(count):
        return jnp.exp(-behind_rate * count)

    low_end, high_end, low_start, high_start = ends[0], ends[1], ends[2], ends[3]
    block_end = high_end + ahead_by(half) * low_end
    block_start = low_start + behind_by(half) * high_start
    u = g % 4
    both = jnp.concatenate([block_end, block_start], axis=0)
    message = both.astype(BF16)
    earlier = jnp.zeros((NP, channels), F32)
    later = jnp.zeros((NP, channels), F32)
    row_end = ahead_by(points * (3 - u)) * block_end
    row_start = behind_by(points * u) * block_start
    for bits in (1, 2, 3):
        came = flip(message, bits).astype(F32)
        v = u ^ bits
        distance = jnp.abs(u - v) - 1
        before = v < u
        earlier += jnp.where(before, ahead_by(points * distance), 0.0) * came[:NP]
        later += jnp.where(before, 0.0, behind_by(points * distance)) * came[NP:]
        row_end += ahead_by(points * (3 - v)) * came[:NP]
        row_start += behind_by(points * v) * came[NP:]
    row_end, row_start = row_end.astype(BF16), row_start.astype(BF16)
    for shift in (1, 2, 3):
        message = jnp.where(z + shift < 4, row_end, row_start)
        came = lax.ppermute(message, "grid", [(n, (n + 4 * shift) % 16) for n in everyone])
        came = came.astype(F32)
        source = (z - shift) % 4
        before = source < z
        distance = jnp.abs(z - source) - 1
        earlier += jnp.where(before, ahead_by(points * (4 * distance + u)), 0.0) * came
        later += jnp.where(before, 0.0, behind_by(points * (4 * distance + 3 - u))) * came
    upper = x == 1
    earlier = jnp.where(upper, low_end + ahead_by(half) * earlier, earlier)
    later = jnp.where(upper, later, high_start + behind_by(half) * later)

    send, keep = pl.pallas_call(
        functools.partial(finish_kernel, step, pieces),
        out_shape=(
            jax.ShapeDtypeStruct((NC * half, channels // 2), BF16),
            jax.ShapeDtypeStruct((NC * half, channels // 2), F32),
        ),
        in_specs=[SMEM_SPEC] + [VMEM_SPEC] * 10 + [HBM_SPEC] * (1 + pieces),
        out_specs=(VMEM_SPEC,) * 2,
        scratch_shapes=[
            pltpu.VMEM((2 * quad, channels), BF16),
            pltpu.VMEM(((NI + NC) * half, channels), BF16),
            pltpu.VMEM((NP * half, quad), BF16),
            pltpu.VMEM((NI * half, quad), BF16),
            pltpu.VMEM((NP * half, channels), BF16),
            pltpu.VMEM((NC * half, 2 * quad), BF16),
            pltpu.VMEM((NP, half, TILE), F32),
            pltpu.VMEM((NP, half, TILE), F32),
            pltpu.SemaphoreType.DMA((pieces + 1,)),
        ],
        compiler_params=pltpu.CompilerParams(vmem_limit_bytes=48 << 20),
        name="finish",
    )(place, own, other, cont, weight, far_weight, degree, earlier, later, part, phi, harmonic_table, *far)
    came = over_x(send)
    block = 128
    return pl.pallas_call(
        place_kernel,
        grid=(channels // 2 // block,),
        out_shape=jax.ShapeDtypeStruct((channels // 2, NC, points), F32),
        in_specs=[
            SMEM_SPEC,
            pl.BlockSpec((NC * half, block), lambda i: (0, i)),
            pl.BlockSpec((NC * half, block), lambda i: (0, i)),
        ],
        out_specs=pl.BlockSpec((block, NC, points), lambda i: (i, 0, 0)),
        name="place",
    )(place, keep, came)


def solution(mesh):
    small = dict(mesh.shape) == {"orb": 2, "grid": 16}
    return jax.shard_map(
        shards_by_table if small else shards,
        mesh=mesh,
        in_specs=(P("orb", "grid", None), P(None, "grid", None), P("orb", None), P("orb"), P()),
        out_specs=P("orb", None, "grid"),
        check_vma=False,
    )
```

```python
import functools
import math

import jax
import jax.numpy as jnp
from jax import lax
from jax.experimental import pallas as pl
from jax.experimental.pallas import tpu as pltpu
from jax.sharding import PartitionSpec as P

LMAX = 47
LM = 2304


LOG_SPAN = 7.0


def combine(earlier, later):
    return (earlier[0] * later[0], earlier[1] * later[0] + later[1])


def channel_degree(lm_index):
    levels = jnp.arange(1, LMAX + 1, dtype=jnp.int32)
    return jnp.sum((lm_index[:, None] >= levels * levels).astype(jnp.float32), axis=1)


def line_sums(forward_source, backward_source, decay_rate, block_size):
    lead_first, lead_second, count, channels = forward_source.shape
    block_count = count // block_size
    forward_blocks = forward_source.reshape(
        lead_first, lead_second, block_count, block_size, channels
    )
    backward_blocks = backward_source.reshape(
        lead_first, lead_second, block_count, block_size, channels
    )
    forward = forward_blocks
    backward = backward_blocks
    for distance in range(1, block_size):
        factor = jnp.exp(-decay_rate * distance)
        padding = jnp.zeros((lead_first, lead_second, block_count, distance, channels), jnp.float32)
        forward = forward + factor * jnp.concatenate(
            [padding, forward_blocks[:, :, :, : block_size - distance]], axis=3
        )
        backward = backward + factor * jnp.concatenate(
            [backward_blocks[:, :, :, distance:], padding], axis=3
        )
    block_decay = jnp.broadcast_to(
        jnp.exp(-decay_rate * block_size), (lead_first, lead_second, block_count, channels)
    )
    forward_total = lax.associative_scan(
        combine, (block_decay, forward[:, :, :, block_size - 1]), axis=2
    )[1]
    backward_total = lax.associative_scan(
        combine, (block_decay, backward[:, :, :, 0]), reverse=True, axis=2
    )[1]
    boundary = jnp.zeros((lead_first, lead_second, 1, channels), jnp.float32)
    earlier_sum = jnp.concatenate([boundary, forward_total[:, :, : block_count - 1]], axis=2)
    later_sum = jnp.concatenate([backward_total[:, :, 1:], boundary], axis=2)
    offsets = jnp.arange(block_size, dtype=jnp.float32)[:, None]
    forward = forward + jnp.exp(-decay_rate * (offsets + 1.0)) * earlier_sum[:, :, :, None, :]
    backward = (
        backward + jnp.exp(-decay_rate * (block_size - offsets)) * later_sum[:, :, :, None, :]
    )
    shape = forward_source.shape
    return (
        forward.reshape(shape),
        backward.reshape(shape),
        forward_total[:, :, block_count - 1],
        backward_total[:, :, 0],
    )


def local_lines(density, degree, points):
    count = density.shape[2]
    increment = LOG_SPAN / points
    positions = jnp.arange(count, dtype=jnp.int32).astype(jnp.float32)[:, None]
    radius = jnp.exp((positions + 1.0 - points) * increment)
    decay_rate = degree * increment
    source = increment * radius * density
    scaled = increment * density
    forward, backward, forward_end, backward_end = line_sums(
        source, scaled, decay_rate, math.gcd(count, 16)
    )
    return (forward, backward, forward_end, backward_end, radius, scaled, decay_rate)


def finish_potential(forward, backward, radius, scaled, degree):
    factor = 4.0 / (2.0 * degree + 1.0)
    return factor * (forward / radius + backward - scaled)


def shards(orbitals, continuum, harmonic_table, ang_weight, channel_lm):
    analysis = (ang_weight[:, None] * harmonic_table.astype(jnp.float32)).astype(jnp.bfloat16)
    phi_ang = jnp.einsum(
        "al,irl->ira",
        harmonic_table,
        lax.all_gather(orbitals, "orb", axis=0, tiled=True),
        preferred_element_type=jnp.float32,
    ).astype(jnp.bfloat16)
    continuum_angular = jnp.einsum(
        "al,krl->kra", harmonic_table, continuum, preferred_element_type=jnp.float32
    ).astype(jnp.bfloat16)
    pair_values = (
        phi_ang.astype(jnp.float32)[:, None] * continuum_angular.astype(jnp.float32)[None]
    ).astype(jnp.bfloat16)
    density = lax.psum_scatter(
        jnp.einsum(
            "al,ikra->ikrl", analysis, pair_values, preferred_element_type=jnp.float32
        ).astype(jnp.bfloat16),
        "orb",
        scatter_dimension=0,
        tiled=True,
    )
    local_count = LM // lax.axis_size("grid")
    local_channel_index = lax.dynamic_slice_in_dim(
        channel_lm, lax.axis_index("grid") * local_count, local_count
    )
    degree = channel_degree(local_channel_index)
    line_density = lax.all_to_all(density, "grid", split_axis=3, concat_axis=2, tiled=True)
    points = line_density.shape[2]
    forward, backward, forward_end, backward_end, radius, scaled, decay_rate = local_lines(
        line_density.astype(jnp.float32), degree, points
    )
    potential = finish_potential(forward, backward, radius, scaled, degree).astype(jnp.bfloat16)
    radial_potential = lax.all_to_all(potential, "grid", split_axis=2, concat_axis=3, tiled=True)
    pot_ang = jnp.einsum(
        "al,ikrl->ikra",
        harmonic_table,
        lax.all_gather(radial_potential, "orb", axis=0, tiled=True),
        preferred_element_type=jnp.float32,
    )
    weighted_values = jnp.sum(phi_ang.astype(jnp.float32)[:, None] * pot_ang, axis=0)
    product = weighted_values.astype(jnp.bfloat16)
    return -lax.psum_scatter(
        jnp.einsum("al,kra->lkr", analysis, product, preferred_element_type=jnp.float32),
        "orb",
        scatter_dimension=0,
        tiled=True,
    )


NC = 4
NI = 2
NP = NI * NC
CHUNK = 256
TILE = 768
F32 = jnp.float32
BF16 = jnp.bfloat16


def dot_nt(a, b):
    return lax.dot_general(a, b, (((1,), (1,)), ((), ())), preferred_element_type=F32)


def dot_nn(a, b):
    return jnp.dot(a, b, preferred_element_type=F32)


def span_of(index, size):
    return pl.ds(pl.multiple_of(index * size, size), size)


def store_pairs(values, weight, points, pairs, span):
    phi = values[: NI * points].astype(F32) * weight
    psi = values[NI * points :].astype(F32)
    for i in range(NI):
        for k in range(NC):
            product = phi[i * points : (i + 1) * points] * psi[k * points : (k + 1) * points]
            row = (i * NC + k) * points
            pairs[row : row + points, span] = product.astype(BF16)


def angular_density(step, x, values_of, store, table, weight, degree_ref, part_ref, ends_at, pairs, work):
    half = part_ref.shape[0] // NC
    points = 2 * half
    steps = table.shape[0] // CHUNK

    def angular(i, carry):
        span = span_of(i, CHUNK)
        phi, psi = values_of(i, span)
        low_high = phi.reshape(2, half, CHUNK)
        store(span, jnp.where(x == 0, low_high[0], low_high[1]), psi)
        phi = phi.astype(F32) * weight[:, span]
        psi = psi.astype(F32)
        for k in range(NC):
            rows = slice(k * points, (k + 1) * points)
            pairs[rows, span] = (phi * psi[rows]).astype(BF16)
        return carry

    lax.fori_loop(0, steps, angular, 0)

    def density(t, carry):
        span = span_of(t, TILE)
        degree = degree_ref[:, span]
        work[...] = dot_nn(pairs[...], table[:, span])
        position = lax.broadcasted_iota(jnp.int32, (half, TILE), 0).astype(F32)
        ahead = jnp.exp((degree + 1.0) * step * (position - (half - 1.0)))
        behind = jnp.exp(-degree * step * position)
        for k in range(NC):
            low = work[k * points : k * points + half, :]
            high = work[k * points + half : (k + 1) * points, :]
            part_ref[k * half : (k + 1) * half, span] = jnp.where(x == 0, low, high).astype(BF16)
            ends = (low * ahead, high * ahead, low * behind, high * behind)
            for n in range(4):
                ends_at(n, k, span, jnp.sum(ends[n], axis=0, keepdims=True))
        return carry

    lax.fori_loop(0, table.shape[1] // TILE, density, 0)


def own_kernel(
    step, place, own, cont, weight, degree_ref, table_hbm,
    part_ref, phi_ref, psi_ref, ends_ref, table,
    rows, pairs, work, sems,
):
    points = own.shape[0]
    steps = table.shape[0] // CHUNK

    def fetch(i):
        return pltpu.make_async_copy(
            table_hbm.at[span_of(i, CHUNK)], table.at[span_of(i, CHUNK)], sems.at[i]
        )

    for i in range(steps):
        fetch(i).start()
    rows[:points, :] = own[...]
    rows[points:, :] = cont[...]

    def values_of(i, span):
        fetch(i).wait()
        values = dot_nt(rows[...], table[span, :]).astype(BF16)
        return values[:points], values[points:]

    def store(span, phi, psi):
        phi_ref[:, span] = phi
        psi_ref[:, span] = psi

    def ends_at(n, k, span, value):
        ends_ref[n * NC + k : n * NC + k + 1, span] = value

    angular_density(
        step, place[0], values_of, store, table, weight, degree_ref, part_ref, ends_at, pairs, work
    )


def other_kernel(
    step, place, other, psi_ref, weight, degree_ref, own_ends, table,
    part_ref, phi_ref, ends_ref,
    pairs, work,
):
    x = place[0]

    def values_of(i, span):
        return dot_nt(other[...], table[span, :]).astype(BF16), psi_ref[:, span]

    def store(span, phi, psi):
        phi_ref[:, span] = phi

    def ends_at(n, k, span, value):
        ends_ref[pl.ds(n * NP + (1 - x) * NC + k, 1), span] = value

    for n in range(4):
        for k in range(NC):
            ends_ref[pl.ds(n * NP + x * NC + k, 1), :] = own_ends[n * NC + k : n * NC + k + 1, :]
    angular_density(
        step, x, values_of, store, table, weight, degree_ref, part_ref, ends_at, pairs, work
    )


def finish_kernel(
    step, pieces, place, own, other, cont, weight, far_weight, degree_ref, earlier, later,
    part, other_part, phi, other_phi, table_hbm, *refs
):
    far_hbm = refs[:pieces]
    send_ref, keep_ref, table, far_table, rows, pairs, phi_all, pot, product, work, total, sems = refs[pieces:]
    x = place[0]
    points = own.shape[0]
    half = points // 2
    quad, channels = table.shape
    steps = quad // CHUNK

    def fetch_far(n):
        size = far_hbm[n].shape[0]
        start = pl.multiple_of(place[1 + n], quad // 16)
        return pltpu.make_async_copy(far_hbm[n], far_table.at[pl.ds(start, size)], sems.at[n])

    def fetch_rows():
        near = span_of(x, half)
        yield pltpu.make_async_copy(own.at[near], rows.at[near], sems.at[pieces])
        for k in range(NC):
            at = span_of(2 * k + x, half)
            to = pl.ds((NI + k) * half, half)
            yield pltpu.make_async_copy(cont.at[at], rows.at[to], sems.at[pieces + 1 + k])

    fetch_table = pltpu.make_async_copy(table_hbm, table, sems.at[pieces + 1 + NC])
    for copy in fetch_rows():
        copy.start()

    for n in range(pieces):
        fetch_far(n).start()
    phi_all[span_of(x, half), :quad] = phi[...]
    phi_all[span_of(1 - x, half), :quad] = other_phi[...]
    fetch_table.start()
    rows[span_of(1 - x, half), :] = other[span_of(x, half), :]
    for copy in fetch_rows():
        copy.wait()
    for n in range(pieces):
        fetch_far(n).wait()

    def angular(i, carry):
        span = span_of(i, CHUNK)
        values = dot_nt(rows[...], far_table[span, :]).astype(BF16)
        store_pairs(values, far_weight[:, span], half, pairs, span)
        phi_all[:, span_of(i + steps, CHUNK)] = values[: NI * half]
        return carry

    lax.fori_loop(0, steps, angular, 0)

    def radial(t, carry):
        span = span_of(t, TILE)
        degree = degree_ref[:, span]
        shrink_ahead = jnp.exp(-(degree + 1.0) * step)
        shrink_behind = jnp.exp(-degree * step)
        factor = 4.0 * step / (2.0 * degree + 1.0)
        far = dot_nn(pairs[...], far_table[:, span])
        work[...] = far.reshape(NP, half, TILE)
        for start, values in ((x * NC, part), (NC - x * NC, other_part)):
            near = values[:, span].astype(F32).reshape(NC, half, TILE)
            work[pl.ds(start, NC)] = work[pl.ds(start, NC)] + near
        ahead = earlier[:, span]
        behind = later[:, span] * shrink_behind
        for j in range(half):
            ahead = ahead * shrink_ahead + work[:, j, :]
            total[:, j, :] = ahead
        for j in range(half - 1, -1, -1):
            total[:, j, :] = factor * (total[:, j, :] + behind)
            behind = (behind + work[:, j, :]) * shrink_behind
        pot[:, span] = total[...].reshape(NP * half, TILE).astype(BF16)
        return carry

    lax.fori_loop(0, channels // TILE, radial, 0)

    def weigh(source, weight_at, first):
        def chunk(i, carry):
            span = span_of(i, CHUNK)
            at = span_of(i + first, CHUNK)
            angle = dot_nt(pot[...], source[span, :])
            values = phi_all[:, at].astype(F32) * weight_at[:, span]
            for k in range(NC):
                value = jnp.zeros((half, CHUNK), F32)
                for o in range(NI):
                    row = (o * NC + k) * half
                    value += values[o * half : (o + 1) * half] * angle[row : row + half]
                product[k * half : (k + 1) * half, at] = value.astype(BF16)
            return carry

        lax.fori_loop(0, steps, chunk, 0)

    weigh(far_table, far_weight, steps)
    fetch_table.wait()
    weigh(table, weight, 0)
    share = channels // 2
    third = share // 3
    for t in range(3):
        away = pl.ds(pl.multiple_of((1 - x) * share + t * third, third), third)
        home = pl.ds(pl.multiple_of(x * share + t * third, third), third)
        columns = slice(t * third, (t + 1) * third)
        for out, place_at in ((send_ref, away), (keep_ref, home)):
            value = dot_nn(product[:, :quad], table[:, place_at])
            value += dot_nn(product[:, quad:], far_table[:, place_at])
            out[:, columns] = (-value).astype(out.dtype)


def slab_kernel(place, table, *refs):
    sems = refs[-1]
    copies = []
    for n, out in enumerate(refs[:-1]):
        start = pl.multiple_of(place[n], 80)
        copies.append(pltpu.make_async_copy(table.at[pl.ds(start, out.shape[0])], out, sems.at[n]))
    for copy in copies:
        copy.start()
    for copy in copies:
        copy.wait()


def place_kernel(place, keep, came, out_ref):
    x = place[0]
    half = keep.shape[0] // NC
    out_ref[:, span_of(x, half), :] = keep[...].reshape(NC, half, -1)
    out_ref[:, span_of(1 - x, half), :] = came[...].astype(F32).reshape(NC, half, -1)


VMEM_SPEC = pl.BlockSpec(memory_space=pltpu.VMEM)
SMEM_SPEC = pl.BlockSpec(memory_space=pltpu.SMEM)
HBM_SPEC = pl.BlockSpec(memory_space=pl.ANY)


def shards_by_table(orbitals, continuum, harmonic_table, ang_weight, channel_lm):
    quad, channels = harmonic_table.shape
    points = orbitals.shape[1]
    half = points // 2
    step = LOG_SPAN / (points * lax.axis_size("grid"))
    x = lax.axis_index("orb")
    g = lax.axis_index("grid")
    core, y, z = g % 2, (g // 2) % 2, g // 4
    across = [(0, 1), (1, 0)]
    everyone = range(16)

    def over_x(value):
        return lax.ppermute(value, "orb", across)

    def flip(value, bits):
        return lax.ppermute(value, "grid", [(n, n ^ bits) for n in everyone])

    pieces = 14
    size = quad // 16
    corner = 2 * (z % 2) + y

    def offset(which, side, n):
        return ((which * 2 + side) * 2 + n) * size

    def after(value, *others):
        return lax.optimization_barrier((value, *others))[0]

    def in_hbm(value):
        return pltpu.with_memory_space_constraint(value, pltpu.HBM)

    hbm = pl.BlockSpec(memory_space=pltpu.HBM)
    slabs = pl.pallas_call(
        slab_kernel,
        out_shape=tuple(jax.ShapeDtypeStruct((n * size, channels), BF16) for n in (1, 1, 2)),
        in_specs=[SMEM_SPEC, hbm],
        out_specs=(VMEM_SPEC,) * 3,
        scratch_shapes=[pltpu.SemaphoreType.DMA((3,))],
        name="slabs",
    )(
        jnp.stack([offset(corner, core, 0), offset(corner, core, 1), offset(corner ^ 3, core, 0)]),
        in_hbm(harmonic_table),
    )

    own = orbitals[0]
    weight = ang_weight[None, :]
    degree = channel_degree(channel_lm)[None, :]
    cont = continuum.reshape(NC * points, channels)
    place = jnp.stack([x]).astype(jnp.int32)
    part_shape = jax.ShapeDtypeStruct((NC * half, channels), BF16)
    phi_shape = jax.ShapeDtypeStruct((half, quad), BF16)

    other = over_x(own)
    first_a = over_x(slabs[0])
    first_b = over_x(slabs[1])
    last = over_x(slabs[2])
    part, phi, psi, own_ends, table = pl.pallas_call(
        functools.partial(own_kernel, step),
        out_shape=(
            part_shape,
            phi_shape,
            jax.ShapeDtypeStruct((NC * points, quad), BF16),
            jax.ShapeDtypeStruct((4 * NC, channels), F32),
            jax.ShapeDtypeStruct((quad, channels), BF16),
        ),
        in_specs=[SMEM_SPEC] + [VMEM_SPEC] * 4 + [pl.BlockSpec(memory_space=pltpu.HBM)],
        out_specs=(VMEM_SPEC,) * 5,
        scratch_shapes=[
            pltpu.VMEM(((1 + NC) * points, channels), BF16),
            pltpu.VMEM((NC * points, quad), BF16),
            pltpu.VMEM((NC * points, TILE), F32),
            pltpu.SemaphoreType.DMA((quad // CHUNK,)),
        ],
        compiler_params=pltpu.CompilerParams(vmem_limit_bytes=16 << 20),
        name="own_orbital",
    )(place, own, cont, weight, degree, in_hbm(after(harmonic_table, slabs[0])))
    other_part, other_phi, ends = pl.pallas_call(
        functools.partial(other_kernel, step),
        out_shape=(part_shape, phi_shape, jax.ShapeDtypeStruct((4 * NP, channels), F32)),
        in_specs=[SMEM_SPEC] + [VMEM_SPEC] * 6,
        out_specs=(VMEM_SPEC,) * 3,
        scratch_shapes=[
            pltpu.VMEM((NC * points, quad), BF16),
            pltpu.VMEM((NC * points, TILE), F32),
        ],
        compiler_params=pltpu.CompilerParams(vmem_limit_bytes=8 << 20),
        name="other_orbital",
    )(place, other, psi, weight, degree, own_ends, table)
    ends = ends.reshape(4, NP, channels)
    ahead_rate = (degree + 1.0) * step
    behind_rate = degree * step

    def ahead_by(count):
        return jnp.exp(-ahead_rate * count)

    def behind_by(count):
        return jnp.exp(-behind_rate * count)

    low_end, high_end, low_start, high_start = ends[0], ends[1], ends[2], ends[3]
    block_end = high_end + ahead_by(half) * low_end
    block_start = low_start + behind_by(half) * high_start
    u = g % 4
    both = jnp.concatenate([block_end, block_start], axis=0)
    message = both.astype(BF16)
    first_a = after(first_a, message)
    earlier = jnp.zeros((NP, channels), F32)
    later = jnp.zeros((NP, channels), F32)
    row_end = ahead_by(points * (3 - u)) * block_end
    row_start = behind_by(points * u) * block_start
    for bits in (1, 2, 3):
        came = flip(message, bits).astype(F32)
        v = u ^ bits
        distance = jnp.abs(u - v) - 1
        before = v < u
        earlier += jnp.where(before, ahead_by(points * distance), 0.0) * came[:NP]
        later += jnp.where(before, 0.0, behind_by(points * distance)) * came[NP:]
        row_end += ahead_by(points * (3 - v)) * came[:NP]
        row_start += behind_by(points * v) * came[NP:]
    row_end = after(row_end.astype(BF16), first_a, first_b)
    row_start = after(row_start.astype(BF16), first_a, first_b)
    for shift in (1, 2, 3):
        message = jnp.where(z + shift < 4, row_end, row_start)
        came = lax.ppermute(message, "grid", [(n, (n + 4 * shift) % 16) for n in everyone])
        came = came.astype(F32)
        source = (z - shift) % 4
        before = source < z
        distance = jnp.abs(z - source) - 1
        earlier += jnp.where(before, ahead_by(points * (4 * distance + u)), 0.0) * came
        later += jnp.where(before, 0.0, behind_by(points * (4 * distance + 3 - u))) * came
    upper_earlier = low_end + ahead_by(half) * earlier
    lower_later = high_start + behind_by(half) * later
    theirs = jnp.concatenate(
        [jnp.where(x == 0, upper_earlier, earlier), jnp.where(x == 0, later, lower_later)], axis=0
    )
    theirs = after(theirs.astype(BF16), last)
    came = over_x(theirs).astype(F32)
    earlier = jnp.where(x == 0, earlier, upper_earlier) + came[:NP]
    later = jnp.where(x == 0, lower_later, later) + came[NP:]
    first_b = after(first_b, row_end)
    received = [first_a, first_b, last]
    received += [flip(first_a, 2), flip(first_a, 4), flip(first_b, 2), flip(first_b, 4)]
    which = [(corner, 0), (corner, 1), (corner ^ 3, 0)]
    which += [(corner ^ 1, 0), (corner ^ 2, 0), (corner ^ 1, 1), (corner ^ 2, 1)]
    far_weight = over_x(after(weight, received[3]))
    far = received + [flip(value, 1) for value in received]
    offsets = [offset(w, core, n) for w, n in which] + [offset(w, 1 - core, n) for w, n in which]
    places = jnp.stack([x] + offsets).astype(jnp.int32)

    send, keep = pl.pallas_call(
        functools.partial(finish_kernel, step, pieces),
        out_shape=(
            jax.ShapeDtypeStruct((NC * half, channels // 2), BF16),
            jax.ShapeDtypeStruct((NC * half, channels // 2), F32),
        ),
        in_specs=[SMEM_SPEC, hbm, VMEM_SPEC, hbm] + [VMEM_SPEC] * 9 + [hbm] + [HBM_SPEC] * pieces,
        out_specs=(VMEM_SPEC,) * 2,
        scratch_shapes=[
            pltpu.VMEM((quad, channels), BF16),
            pltpu.VMEM((quad, channels), BF16),
            pltpu.VMEM(((NI + NC) * half, channels), BF16),
            pltpu.VMEM((NP * half, quad), BF16),
            pltpu.VMEM((NI * half, 2 * quad), BF16),
            pltpu.VMEM((NP * half, channels), BF16),
            pltpu.VMEM((NC * half, 2 * quad), BF16),
            pltpu.VMEM((NP, half, TILE), F32),
            pltpu.VMEM((NP, half, TILE), F32),
            pltpu.SemaphoreType.DMA((pieces + 2 + NC,)),
        ],
        compiler_params=pltpu.CompilerParams(vmem_limit_bytes=26 << 20),
        name="finish",
    )(
        places, in_hbm(own), other, in_hbm(cont), weight, far_weight, degree, earlier, later,
        part, other_part, phi, other_phi, in_hbm(harmonic_table), *far,
    )
    came = over_x(send)
    out = pl.pallas_call(
        place_kernel,
        out_shape=jax.ShapeDtypeStruct((NC, points, channels // 2), F32),
        in_specs=[SMEM_SPEC, VMEM_SPEC, VMEM_SPEC],
        out_specs=VMEM_SPEC,
        name="place",
    )(place, keep, came)
    return jnp.transpose(out, (2, 0, 1))


def solution(mesh):
    small = dict(mesh.shape) == {"orb": 2, "grid": 16}
    return jax.shard_map(
        shards_by_table if small else shards,
        mesh=mesh,
        in_specs=(P("orb", "grid", None), P(None, "grid", None), P("orb", None), P("orb"), P()),
        out_specs=P("orb", None, "grid"),
        check_vma=False,
    )
```

```python
import functools
import math

import jax
import jax.numpy as jnp
from jax import lax
from jax.experimental import pallas as pl
from jax.experimental.pallas import tpu as pltpu
from jax.sharding import PartitionSpec as P

LMAX = 47
LM = 2304


LOG_SPAN = 7.0


def combine(earlier, later):
    return (earlier[0] * later[0], earlier[1] * later[0] + later[1])


def channel_degree(lm_index):
    levels = jnp.arange(1, LMAX + 1, dtype=jnp.int32)
    return jnp.sum((lm_index[:, None] >= levels * levels).astype(jnp.float32), axis=1)


def line_sums(forward_source, backward_source, decay_rate, block_size):
    lead_first, lead_second, count, channels = forward_source.shape
    block_count = count // block_size
    forward_blocks = forward_source.reshape(
        lead_first, lead_second, block_count, block_size, channels
    )
    backward_blocks = backward_source.reshape(
        lead_first, lead_second, block_count, block_size, channels
    )
    forward = forward_blocks
    backward = backward_blocks
    for distance in range(1, block_size):
        factor = jnp.exp(-decay_rate * distance)
        padding = jnp.zeros((lead_first, lead_second, block_count, distance, channels), jnp.float32)
        forward = forward + factor * jnp.concatenate(
            [padding, forward_blocks[:, :, :, : block_size - distance]], axis=3
        )
        backward = backward + factor * jnp.concatenate(
            [backward_blocks[:, :, :, distance:], padding], axis=3
        )
    block_decay = jnp.broadcast_to(
        jnp.exp(-decay_rate * block_size), (lead_first, lead_second, block_count, channels)
    )
    forward_total = lax.associative_scan(
        combine, (block_decay, forward[:, :, :, block_size - 1]), axis=2
    )[1]
    backward_total = lax.associative_scan(
        combine, (block_decay, backward[:, :, :, 0]), reverse=True, axis=2
    )[1]
    boundary = jnp.zeros((lead_first, lead_second, 1, channels), jnp.float32)
    earlier_sum = jnp.concatenate([boundary, forward_total[:, :, : block_count - 1]], axis=2)
    later_sum = jnp.concatenate([backward_total[:, :, 1:], boundary], axis=2)
    offsets = jnp.arange(block_size, dtype=jnp.float32)[:, None]
    forward = forward + jnp.exp(-decay_rate * (offsets + 1.0)) * earlier_sum[:, :, :, None, :]
    backward = (
        backward + jnp.exp(-decay_rate * (block_size - offsets)) * later_sum[:, :, :, None, :]
    )
    shape = forward_source.shape
    return (
        forward.reshape(shape),
        backward.reshape(shape),
        forward_total[:, :, block_count - 1],
        backward_total[:, :, 0],
    )


def local_lines(density, degree, points):
    count = density.shape[2]
    increment = LOG_SPAN / points
    positions = jnp.arange(count, dtype=jnp.int32).astype(jnp.float32)[:, None]
    radius = jnp.exp((positions + 1.0 - points) * increment)
    decay_rate = degree * increment
    source = increment * radius * density
    scaled = increment * density
    forward, backward, forward_end, backward_end = line_sums(
        source, scaled, decay_rate, math.gcd(count, 16)
    )
    return (forward, backward, forward_end, backward_end, radius, scaled, decay_rate)


def finish_potential(forward, backward, radius, scaled, degree):
    factor = 4.0 / (2.0 * degree + 1.0)
    return factor * (forward / radius + backward - scaled)


def shards(orbitals, continuum, harmonic_table, ang_weight, channel_lm):
    analysis = (ang_weight[:, None] * harmonic_table.astype(jnp.float32)).astype(jnp.bfloat16)
    phi_ang = jnp.einsum(
        "al,irl->ira",
        harmonic_table,
        lax.all_gather(orbitals, "orb", axis=0, tiled=True),
        preferred_element_type=jnp.float32,
    ).astype(jnp.bfloat16)
    continuum_angular = jnp.einsum(
        "al,krl->kra", harmonic_table, continuum, preferred_element_type=jnp.float32
    ).astype(jnp.bfloat16)
    pair_values = (
        phi_ang.astype(jnp.float32)[:, None] * continuum_angular.astype(jnp.float32)[None]
    ).astype(jnp.bfloat16)
    density = lax.psum_scatter(
        jnp.einsum(
            "al,ikra->ikrl", analysis, pair_values, preferred_element_type=jnp.float32
        ).astype(jnp.bfloat16),
        "orb",
        scatter_dimension=0,
        tiled=True,
    )
    local_count = LM // lax.axis_size("grid")
    local_channel_index = lax.dynamic_slice_in_dim(
        channel_lm, lax.axis_index("grid") * local_count, local_count
    )
    degree = channel_degree(local_channel_index)
    line_density = lax.all_to_all(density, "grid", split_axis=3, concat_axis=2, tiled=True)
    points = line_density.shape[2]
    forward, backward, forward_end, backward_end, radius, scaled, decay_rate = local_lines(
        line_density.astype(jnp.float32), degree, points
    )
    potential = finish_potential(forward, backward, radius, scaled, degree).astype(jnp.bfloat16)
    radial_potential = lax.all_to_all(potential, "grid", split_axis=2, concat_axis=3, tiled=True)
    pot_ang = jnp.einsum(
        "al,ikrl->ikra",
        harmonic_table,
        lax.all_gather(radial_potential, "orb", axis=0, tiled=True),
        preferred_element_type=jnp.float32,
    )
    weighted_values = jnp.sum(phi_ang.astype(jnp.float32)[:, None] * pot_ang, axis=0)
    product = weighted_values.astype(jnp.bfloat16)
    return -lax.psum_scatter(
        jnp.einsum("al,kra->lkr", analysis, product, preferred_element_type=jnp.float32),
        "orb",
        scatter_dimension=0,
        tiled=True,
    )


NC = 4
NI = 2
NP = NI * NC
CHUNK = 256
WIDE = 640
TILE = 768
F32 = jnp.float32
BF16 = jnp.bfloat16


def dot_nt(a, b):
    return lax.dot_general(a, b, (((1,), (1,)), ((), ())), preferred_element_type=F32)


def dot_nn(a, b):
    return jnp.dot(a, b, preferred_element_type=F32)


def span_of(index, size):
    return pl.ds(pl.multiple_of(index * size, size), size)


def store_pairs(values, weight, points, pairs, span):
    phi = values[: NI * points].astype(F32) * weight
    psi = values[NI * points :].astype(F32)
    for i in range(NI):
        for k in range(NC):
            product = phi[i * points : (i + 1) * points] * psi[k * points : (k + 1) * points]
            row = (i * NC + k) * points
            pairs[row : row + points, span] = product.astype(BF16)


def angular_density(step, x, values_of, store, table, weight, degree_ref, part_ref, ends_at, pairs, work):
    half = part_ref.shape[0] // NC
    points = 2 * half
    steps = table.shape[0] // CHUNK

    def angular(i, carry):
        span = span_of(i, CHUNK)
        phi, psi = values_of(i, span)
        low_high = phi.reshape(2, half, CHUNK)
        store(span, jnp.where(x == 0, low_high[0], low_high[1]), psi)
        phi = phi.astype(F32) * weight[:, span]
        psi = psi.astype(F32)
        for k in range(NC):
            rows = slice(k * points, (k + 1) * points)
            pairs[rows, span] = (phi * psi[rows]).astype(BF16)
        return carry

    lax.fori_loop(0, steps, angular, 0)

    def density(t, carry):
        span = span_of(t, TILE)
        degree = degree_ref[:, span]
        work[...] = dot_nn(pairs[...], table[:, span])
        position = lax.broadcasted_iota(jnp.int32, (half, TILE), 0).astype(F32)
        ahead = jnp.exp((degree + 1.0) * step * (position - (half - 1.0)))
        behind = jnp.exp(-degree * step * position)
        for k in range(NC):
            low = work[k * points : k * points + half, :]
            high = work[k * points + half : (k + 1) * points, :]
            part_ref[k * half : (k + 1) * half, span] = jnp.where(x == 0, low, high).astype(BF16)
            ends = (low * ahead, high * ahead, low * behind, high * behind)
            for n in range(4):
                ends_at(n, k, span, jnp.sum(ends[n], axis=0, keepdims=True))
        return carry

    lax.fori_loop(0, table.shape[1] // TILE, density, 0)


def own_kernel(
    step, place, own, cont, weight, degree_ref, table_hbm,
    part_any, phi_any, psi_ref, ends_ref, table,
    part_ref, phi_ref, rows, pairs, work, sems,
):
    points = own.shape[0]
    steps = table.shape[0] // CHUNK

    def fetch(i):
        return pltpu.make_async_copy(
            table_hbm.at[span_of(i, CHUNK)], table.at[span_of(i, CHUNK)], sems.at[i]
        )

    for i in range(steps):
        fetch(i).start()
    rows[:points, :] = own[...]
    rows[points:, :] = cont[...]

    def values_of(i, span):
        fetch(i).wait()
        values = dot_nt(rows[...], table[span, :]).astype(BF16)
        return values[:points], values[points:]

    def store(span, phi, psi):
        phi_ref[:, span] = phi
        psi_ref[:, span] = psi

    def ends_at(n, k, span, value):
        ends_ref[n * NC + k : n * NC + k + 1, span] = value

    angular_density(
        step, place[0], values_of, store, table, weight, degree_ref, part_ref, ends_at, pairs, work
    )
    copies = [
        pltpu.make_async_copy(part_ref, part_any, sems.at[0]),
        pltpu.make_async_copy(phi_ref, phi_any, sems.at[1]),
    ]
    for copy in copies:
        copy.start()
    for copy in copies:
        copy.wait()


def other_kernel(
    step, place, other, psi_ref, weight, degree_ref, own_ends, table,
    part_any, phi_any, ends_ref, slab_any,
    part_ref, phi_ref, pairs, work, sems,
):
    x = place[0]
    slab = pl.ds(pl.multiple_of(place[1], slab_any.shape[0]), slab_any.shape[0])
    copies = [pltpu.make_async_copy(table.at[slab], slab_any, sems.at[0])]
    copies[0].start()

    def values_of(i, span):
        return dot_nt(other[...], table[span, :]).astype(BF16), psi_ref[:, span]

    def store(span, phi, psi):
        phi_ref[:, span] = phi

    def ends_at(n, k, span, value):
        ends_ref[pl.ds(n * NP + (1 - x) * NC + k, 1), span] = value

    for n in range(4):
        for k in range(NC):
            ends_ref[pl.ds(n * NP + x * NC + k, 1), :] = own_ends[n * NC + k : n * NC + k + 1, :]
    angular_density(
        step, x, values_of, store, table, weight, degree_ref, part_ref, ends_at, pairs, work
    )
    copies.append(pltpu.make_async_copy(part_ref, part_any, sems.at[1]))
    copies.append(pltpu.make_async_copy(phi_ref, phi_any, sems.at[2]))
    for copy in copies[1:]:
        copy.start()
    for copy in copies:
        copy.wait()


def finish_kernel(
    step, pieces, place, own, other, cont, weight, far_weight, degree_ref, earlier, later,
    part_any, other_part_any, phi_any, other_phi_any, table_hbm, *refs
):
    far_hbm = refs[:pieces]
    send_any, keep_any, send_ref, keep_ref, part, table, far_table, rows, pairs, sorted_pairs, phi_all, pot, product, work, total, sems = refs[pieces:]
    x = place[0]
    points = own.shape[0]
    half = points // 2
    quad, channels = table.shape
    steps = quad // WIDE

    def fetch_far(n):
        size = far_hbm[n].shape[0]
        start = pl.multiple_of(place[1 + n], quad // 16)
        return pltpu.make_async_copy(far_hbm[n], far_table.at[pl.ds(start, size)], sems.at[n])

    def fetch_rows():
        near = span_of(x, half)
        yield pltpu.make_async_copy(own.at[near], rows.at[near], sems.at[pieces])
        for k in range(NC):
            at = span_of(2 * k + x, half)
            to = pl.ds((NI + k) * half, half)
            yield pltpu.make_async_copy(cont.at[at], rows.at[to], sems.at[pieces + 1 + k])

    fetch_table = pltpu.make_async_copy(table_hbm, table, sems.at[pieces + 1 + NC])
    for copy in fetch_rows():
        copy.start()

    for n in range(pieces):
        fetch_far(n).start()
    near = [
        pltpu.make_async_copy(phi_any, phi_all.at[span_of(x, half), pl.ds(0, quad)], sems.at[pieces + 2 + NC]),
        pltpu.make_async_copy(other_phi_any, phi_all.at[span_of(1 - x, half), pl.ds(0, quad)], sems.at[pieces + 3 + NC]),
        pltpu.make_async_copy(part_any, part.at[span_of(x, NC * half)], sems.at[pieces + 4 + NC]),
        pltpu.make_async_copy(other_part_any, part.at[span_of(1 - x, NC * half)], sems.at[pieces + 5 + NC]),
    ]
    for copy in near:
        copy.start()
    fetch_table.start()
    rows[span_of(1 - x, half), :] = other[span_of(x, half), :]
    for copy in fetch_rows():
        copy.wait()
    for n in range(pieces):
        fetch_far(n).wait()

    shape = (NP * half, NP * half)
    row, column = (lax.broadcasted_iota(jnp.int32, shape, n) for n in range(2))
    by_point = ((row & (NP - 1)) * half + (row >> 3) == column).astype(F32).astype(BF16)
    by_pair = ((column & (NP - 1)) * half + (column >> 3) == row).astype(F32).astype(BF16)

    def angular(i, carry):
        span = span_of(i, WIDE)
        values = dot_nt(rows[...], far_table[span, :]).astype(BF16)
        store_pairs(values, far_weight[:, span], half, pairs, span)
        phi_all[:, span_of(i + steps, WIDE)] = values[: NI * half]
        sorted_pairs[:, span] = dot_nn(by_point, pairs[:, span]).astype(BF16)
        return carry

    lax.fori_loop(0, steps, angular, 0)
    for copy in near:
        copy.wait()

    def radial(t, carry):
        span = span_of(t, TILE)
        degree = degree_ref[:, span]
        shrink_ahead = jnp.exp(-(degree + 1.0) * step)
        shrink_behind = jnp.exp(-degree * step)
        factor = 4.0 * step / (2.0 * degree + 1.0)
        density = dot_nn(sorted_pairs[...], far_table[:, span]) + dot_nn(by_point, part[:, span])
        work[...] = density.reshape(half, NP, TILE)
        ahead = earlier[:, span]
        behind = later[:, span] * shrink_behind
        for j in range(half):
            ahead = ahead * shrink_ahead + work[j]
            total[j] = ahead
        for j in range(half - 1, -1, -1):
            total[j] = factor * (total[j] + behind)
            behind = (behind + work[j]) * shrink_behind
        potential = total[...].reshape(NP * half, TILE).astype(BF16)
        pot[:, span] = dot_nn(by_pair, potential).astype(BF16)
        return carry

    lax.fori_loop(0, channels // TILE, radial, 0)

    def weigh(source, weight_at, first):
        def chunk(i, carry):
            span = span_of(i, WIDE)
            at = span_of(i + first, WIDE)
            angle = dot_nt(pot[...], source[span, :])
            values = phi_all[:, at].astype(F32) * weight_at[:, span]
            for k in range(NC):
                value = jnp.zeros((half, WIDE), F32)
                for o in range(NI):
                    row = (o * NC + k) * half
                    value += values[o * half : (o + 1) * half] * angle[row : row + half]
                product[k * half : (k + 1) * half, at] = value.astype(BF16)
            return carry

        lax.fori_loop(0, steps, chunk, 0)

    weigh(far_table, far_weight, steps)
    fetch_table.wait()
    weigh(table, weight, 0)
    share = channels // 2
    leave = []
    for n, (out, to, first) in enumerate(
        ((send_ref, send_any, (1 - x) * share), (keep_ref, keep_any, x * share))
    ):
        at = pl.ds(pl.multiple_of(first, share), share)
        value = dot_nn(product[:, :quad], table[:, at]) + dot_nn(product[:, quad:], far_table[:, at])
        out[...] = (-value).astype(out.dtype)
        leave.append(pltpu.make_async_copy(out, to, sems.at[n]))
        leave[n].start()
    for copy in leave:
        copy.wait()


def slab_kernel(place, table, *refs):
    sems = refs[-1]
    copies = []
    for n, out in enumerate(refs[:-1]):
        start = pl.multiple_of(place[n], 80)
        copies.append(pltpu.make_async_copy(table.at[pl.ds(start, out.shape[0])], out, sems.at[n]))
    for copy in copies:
        copy.start()
    for copy in copies:
        copy.wait()


def place_kernel(place, keep, came, out_ref):
    x = place[0]
    half = keep.shape[0] // NC
    out_ref[:, span_of(x, half), :] = keep[...].reshape(NC, half, -1)
    out_ref[:, span_of(1 - x, half), :] = came[...].astype(F32).reshape(NC, half, -1)


VMEM_SPEC = pl.BlockSpec(memory_space=pltpu.VMEM)
SMEM_SPEC = pl.BlockSpec(memory_space=pltpu.SMEM)
HBM_SPEC = pl.BlockSpec(memory_space=pl.ANY)
ANY_SPEC = HBM_SPEC


def shards_by_table(orbitals, continuum, harmonic_table, ang_weight, channel_lm):
    quad, channels = harmonic_table.shape
    points = orbitals.shape[1]
    half = points // 2
    step = LOG_SPAN / (points * lax.axis_size("grid"))
    x = lax.axis_index("orb")
    g = lax.axis_index("grid")
    core, y, z = g % 2, (g // 2) % 2, g // 4
    across = [(0, 1), (1, 0)]
    everyone = range(16)

    def over_x(value):
        return lax.ppermute(value, "orb", across)

    def flip(value, bits):
        return lax.ppermute(value, "grid", [(n, n ^ bits) for n in everyone])

    pieces = 14
    size = quad // 16
    corner = 2 * (z % 2) + y

    def offset(which, side, n):
        return ((which * 2 + side) * 2 + n) * size

    def after(value, *others):
        return lax.optimization_barrier((value, *others))[0]

    def in_hbm(value):
        return pltpu.with_memory_space_constraint(value, pltpu.HBM)

    hbm = pl.BlockSpec(memory_space=pltpu.HBM)
    slabs = pl.pallas_call(
        slab_kernel,
        out_shape=tuple(jax.ShapeDtypeStruct((n * size, channels), BF16) for n in (1, 2)),
        in_specs=[SMEM_SPEC, hbm],
        out_specs=(VMEM_SPEC,) * 2,
        scratch_shapes=[pltpu.SemaphoreType.DMA((2,))],
        name="slabs",
    )(
        jnp.stack([offset(corner, core, 0), offset(corner ^ 3, core, 0)]),
        in_hbm(harmonic_table),
    )

    own = orbitals[0]
    weight = ang_weight[None, :]
    degree = channel_degree(channel_lm)[None, :]
    cont = continuum.reshape(NC * points, channels)
    place = jnp.stack([x, offset(corner, core, 1)]).astype(jnp.int32)
    part_shape = jax.ShapeDtypeStruct((NC * half, channels), BF16)
    phi_shape = jax.ShapeDtypeStruct((half, quad), BF16)

    other = over_x(own)
    first_a = over_x(slabs[0])
    last = over_x(slabs[1])
    part, phi, psi, own_ends, table = pl.pallas_call(
        functools.partial(own_kernel, step),
        out_shape=(
            part_shape,
            phi_shape,
            jax.ShapeDtypeStruct((NC * points, quad), BF16),
            jax.ShapeDtypeStruct((4 * NC, channels), F32),
            jax.ShapeDtypeStruct((quad, channels), BF16),
        ),
        in_specs=[SMEM_SPEC] + [VMEM_SPEC] * 4 + [pl.BlockSpec(memory_space=pltpu.HBM)],
        out_specs=(ANY_SPEC,) * 2 + (VMEM_SPEC,) * 3,
        scratch_shapes=[
            pltpu.VMEM((NC * half, channels), BF16),
            pltpu.VMEM((half, quad), BF16),
            pltpu.VMEM(((1 + NC) * points, channels), BF16),
            pltpu.VMEM((NC * points, quad), BF16),
            pltpu.VMEM((NC * points, TILE), F32),
            pltpu.SemaphoreType.DMA((quad // CHUNK,)),
        ],
        compiler_params=pltpu.CompilerParams(vmem_limit_bytes=16 << 20),
        name="own_orbital",
    )(place, own, cont, weight, degree, in_hbm(after(harmonic_table, slabs[0])))
    other_part, other_phi, ends, slab = pl.pallas_call(
        functools.partial(other_kernel, step),
        out_shape=(
            part_shape,
            phi_shape,
            jax.ShapeDtypeStruct((4 * NP, channels), F32),
            jax.ShapeDtypeStruct((size, channels), BF16),
        ),
        in_specs=[SMEM_SPEC] + [VMEM_SPEC] * 6,
        out_specs=(ANY_SPEC, ANY_SPEC, VMEM_SPEC, ANY_SPEC),
        scratch_shapes=[
            pltpu.VMEM((NC * half, channels), BF16),
            pltpu.VMEM((half, quad), BF16),
            pltpu.VMEM((NC * points, quad), BF16),
            pltpu.VMEM((NC * points, TILE), F32),
            pltpu.SemaphoreType.DMA((3,)),
        ],
        compiler_params=pltpu.CompilerParams(vmem_limit_bytes=8 << 20),
        name="other_orbital",
    )(place, other, psi, weight, degree, own_ends, table)
    ends = ends.reshape(4, NP, channels)
    ahead_rate = (degree + 1.0) * step
    behind_rate = degree * step

    def ahead_by(count):
        return jnp.exp(-ahead_rate * count)

    def behind_by(count):
        return jnp.exp(-behind_rate * count)

    low_end, high_end, low_start, high_start = ends[0], ends[1], ends[2], ends[3]
    block_end = high_end + ahead_by(half) * low_end
    block_start = low_start + behind_by(half) * high_start
    u = g % 4
    both = jnp.concatenate([block_end, block_start], axis=0)
    message = both.astype(BF16)
    first_a = after(first_a, message)
    earlier = jnp.zeros((NP, channels), F32)
    later = jnp.zeros((NP, channels), F32)
    row_end = ahead_by(points * (3 - u)) * block_end
    row_start = behind_by(points * u) * block_start
    for bits in (1, 2, 3):
        came = flip(message, bits).astype(F32)
        v = u ^ bits
        distance = jnp.abs(u - v) - 1
        before = v < u
        earlier += jnp.where(before, ahead_by(points * distance), 0.0) * came[:NP]
        later += jnp.where(before, 0.0, behind_by(points * distance)) * came[NP:]
        row_end += ahead_by(points * (3 - v)) * came[:NP]
        row_start += behind_by(points * v) * came[NP:]
    row_end = after(row_end.astype(BF16), first_a, last)
    row_start = after(row_start.astype(BF16), first_a, last)
    first_b = over_x(after(slab, row_end))
    for shift in (1, 2, 3):
        message = jnp.where(z + shift < 4, row_end, row_start)
        came = lax.ppermute(message, "grid", [(n, (n + 4 * shift) % 16) for n in everyone])
        came = came.astype(F32)
        source = (z - shift) % 4
        before = source < z
        distance = jnp.abs(z - source) - 1
        earlier += jnp.where(before, ahead_by(points * (4 * distance + u)), 0.0) * came
        later += jnp.where(before, 0.0, behind_by(points * (4 * distance + 3 - u))) * came
    upper_earlier = low_end + ahead_by(half) * earlier
    lower_later = high_start + behind_by(half) * later
    theirs = jnp.concatenate(
        [jnp.where(x == 0, upper_earlier, earlier), jnp.where(x == 0, later, lower_later)], axis=0
    )
    terms, rest = [], weight
    for _ in range(3):
        terms.append(lax.reduce_precision(rest, 8, 7))
        rest = rest - terms[-1]
    terms = jnp.pad(jnp.concatenate(terms, axis=0), ((0, NP - 3), (0, channels - quad)))
    theirs = jnp.concatenate([theirs, terms], axis=0)
    theirs = theirs.astype(BF16)
    came = over_x(theirs).astype(F32)
    far_weight = jnp.sum(came[2 * NP : 2 * NP + 3, :quad], axis=0, keepdims=True)
    earlier = jnp.where(x == 0, earlier, upper_earlier) + came[:NP]
    later = jnp.where(x == 0, lower_later, later) + came[NP : 2 * NP]
    first_b = after(first_b, theirs)
    received = [first_a, first_b, last]
    received += [flip(first_a, 2), flip(first_a, 4), flip(first_b, 2), flip(first_b, 4)]
    which = [(corner, 0), (corner, 1), (corner ^ 3, 0)]
    which += [(corner ^ 1, 0), (corner ^ 2, 0), (corner ^ 1, 1), (corner ^ 2, 1)]
    far = received + [flip(value, 1) for value in received]
    offsets = [offset(w, core, n) for w, n in which] + [offset(w, 1 - core, n) for w, n in which]
    places = jnp.stack([x] + offsets).astype(jnp.int32)

    send, keep = pl.pallas_call(
        functools.partial(finish_kernel, step, pieces),
        out_shape=(
            jax.ShapeDtypeStruct((NC * half, channels // 2), BF16),
            jax.ShapeDtypeStruct((NC * half, channels // 2), F32),
        ),
        in_specs=[SMEM_SPEC, hbm, VMEM_SPEC, hbm] + [VMEM_SPEC] * 5 + [ANY_SPEC] * 4 + [hbm] + [HBM_SPEC] * pieces,
        out_specs=(ANY_SPEC,) * 2,
        scratch_shapes=[
            pltpu.VMEM((NC * half, channels // 2), BF16),
            pltpu.VMEM((NC * half, channels // 2), F32),
            pltpu.VMEM((NP * half, channels), BF16),
            pltpu.VMEM((quad, channels), BF16),
            pltpu.VMEM((quad, channels), BF16),
            pltpu.VMEM(((NI + NC) * half, channels), BF16),
            pltpu.VMEM((NP * half, quad), BF16),
            pltpu.VMEM((NP * half, quad), BF16),
            pltpu.VMEM((NI * half, 2 * quad), BF16),
            pltpu.VMEM((NP * half, channels), BF16),
            pltpu.VMEM((NC * half, 2 * quad), BF16),
            pltpu.VMEM((half, NP, TILE), F32),
            pltpu.VMEM((half, NP, TILE), F32),
            pltpu.SemaphoreType.DMA((pieces + 6 + NC,)),
        ],
        compiler_params=pltpu.CompilerParams(vmem_limit_bytes=30 << 20),
        name="finish",
    )(
        places, in_hbm(own), other, in_hbm(cont), weight, far_weight, degree, earlier, later,
        part, other_part, phi, other_phi, in_hbm(harmonic_table), *far,
    )
    came = over_x(send)
    out = pl.pallas_call(
        place_kernel,
        out_shape=jax.ShapeDtypeStruct((NC, points, channels // 2), F32),
        in_specs=[SMEM_SPEC, VMEM_SPEC, VMEM_SPEC],
        out_specs=VMEM_SPEC,
        name="place",
    )(place, keep, came)
    return jnp.transpose(out, (2, 0, 1))


def solution(mesh):
    small = dict(mesh.shape) == {"orb": 2, "grid": 16}
    return jax.shard_map(
        shards_by_table if small else shards,
        mesh=mesh,
        in_specs=(P("orb", "grid", None), P(None, "grid", None), P("orb", None), P("orb"), P()),
        out_specs=P("orb", None, "grid"),
        check_vma=False,
    )
```

```python
import functools
import math

import jax
import jax.numpy as jnp
from jax import lax
from jax.experimental import pallas as pl
from jax.experimental.pallas import tpu as pltpu
from jax.sharding import PartitionSpec as P

LMAX = 47
LM = 2304


LOG_SPAN = 7.0


def combine(earlier, later):
    return (earlier[0] * later[0], earlier[1] * later[0] + later[1])


def channel_degree(lm_index):
    levels = jnp.arange(1, LMAX + 1, dtype=jnp.int32)
    return jnp.sum((lm_index[:, None] >= levels * levels).astype(jnp.float32), axis=1)


def line_sums(forward_source, backward_source, decay_rate, block_size):
    lead_first, lead_second, count, channels = forward_source.shape
    block_count = count // block_size
    forward_blocks = forward_source.reshape(
        lead_first, lead_second, block_count, block_size, channels
    )
    backward_blocks = backward_source.reshape(
        lead_first, lead_second, block_count, block_size, channels
    )
    forward = forward_blocks
    backward = backward_blocks
    for distance in range(1, block_size):
        factor = jnp.exp(-decay_rate * distance)
        padding = jnp.zeros((lead_first, lead_second, block_count, distance, channels), jnp.float32)
        forward = forward + factor * jnp.concatenate(
            [padding, forward_blocks[:, :, :, : block_size - distance]], axis=3
        )
        backward = backward + factor * jnp.concatenate(
            [backward_blocks[:, :, :, distance:], padding], axis=3
        )
    block_decay = jnp.broadcast_to(
        jnp.exp(-decay_rate * block_size), (lead_first, lead_second, block_count, channels)
    )
    forward_total = lax.associative_scan(
        combine, (block_decay, forward[:, :, :, block_size - 1]), axis=2
    )[1]
    backward_total = lax.associative_scan(
        combine, (block_decay, backward[:, :, :, 0]), reverse=True, axis=2
    )[1]
    boundary = jnp.zeros((lead_first, lead_second, 1, channels), jnp.float32)
    earlier_sum = jnp.concatenate([boundary, forward_total[:, :, : block_count - 1]], axis=2)
    later_sum = jnp.concatenate([backward_total[:, :, 1:], boundary], axis=2)
    offsets = jnp.arange(block_size, dtype=jnp.float32)[:, None]
    forward = forward + jnp.exp(-decay_rate * (offsets + 1.0)) * earlier_sum[:, :, :, None, :]
    backward = (
        backward + jnp.exp(-decay_rate * (block_size - offsets)) * later_sum[:, :, :, None, :]
    )
    shape = forward_source.shape
    return (
        forward.reshape(shape),
        backward.reshape(shape),
        forward_total[:, :, block_count - 1],
        backward_total[:, :, 0],
    )


def local_lines(density, degree, points):
    count = density.shape[2]
    increment = LOG_SPAN / points
    positions = jnp.arange(count, dtype=jnp.int32).astype(jnp.float32)[:, None]
    radius = jnp.exp((positions + 1.0 - points) * increment)
    decay_rate = degree * increment
    source = increment * radius * density
    scaled = increment * density
    forward, backward, forward_end, backward_end = line_sums(
        source, scaled, decay_rate, math.gcd(count, 16)
    )
    return (forward, backward, forward_end, backward_end, radius, scaled, decay_rate)


def finish_potential(forward, backward, radius, scaled, degree):
    factor = 4.0 / (2.0 * degree + 1.0)
    return factor * (forward / radius + backward - scaled)


def shards(orbitals, continuum, harmonic_table, ang_weight, channel_lm):
    analysis = (ang_weight[:, None] * harmonic_table.astype(jnp.float32)).astype(jnp.bfloat16)
    phi_ang = jnp.einsum(
        "al,irl->ira",
        harmonic_table,
        lax.all_gather(orbitals, "orb", axis=0, tiled=True),
        preferred_element_type=jnp.float32,
    ).astype(jnp.bfloat16)
    continuum_angular = jnp.einsum(
        "al,krl->kra", harmonic_table, continuum, preferred_element_type=jnp.float32
    ).astype(jnp.bfloat16)
    pair_values = (
        phi_ang.astype(jnp.float32)[:, None] * continuum_angular.astype(jnp.float32)[None]
    ).astype(jnp.bfloat16)
    density = lax.psum_scatter(
        jnp.einsum(
            "al,ikra->ikrl", analysis, pair_values, preferred_element_type=jnp.float32
        ).astype(jnp.bfloat16),
        "orb",
        scatter_dimension=0,
        tiled=True,
    )
    local_count = LM // lax.axis_size("grid")
    local_channel_index = lax.dynamic_slice_in_dim(
        channel_lm, lax.axis_index("grid") * local_count, local_count
    )
    degree = channel_degree(local_channel_index)
    line_density = lax.all_to_all(density, "grid", split_axis=3, concat_axis=2, tiled=True)
    points = line_density.shape[2]
    forward, backward, forward_end, backward_end, radius, scaled, decay_rate = local_lines(
        line_density.astype(jnp.float32), degree, points
    )
    potential = finish_potential(forward, backward, radius, scaled, degree).astype(jnp.bfloat16)
    radial_potential = lax.all_to_all(potential, "grid", split_axis=2, concat_axis=3, tiled=True)
    pot_ang = jnp.einsum(
        "al,ikrl->ikra",
        harmonic_table,
        lax.all_gather(radial_potential, "orb", axis=0, tiled=True),
        preferred_element_type=jnp.float32,
    )
    weighted_values = jnp.sum(phi_ang.astype(jnp.float32)[:, None] * pot_ang, axis=0)
    product = weighted_values.astype(jnp.bfloat16)
    return -lax.psum_scatter(
        jnp.einsum("al,kra->lkr", analysis, product, preferred_element_type=jnp.float32),
        "orb",
        scatter_dimension=0,
        tiled=True,
    )


NC = 4
NI = 2
NP = NI * NC
CHUNK = 256
WIDE = 640
TILE = 768
F32 = jnp.float32
BF16 = jnp.bfloat16


def dot_nt(a, b):
    return lax.dot_general(a, b, (((1,), (1,)), ((), ())), preferred_element_type=F32)


def dot_nn(a, b):
    return jnp.dot(a, b, preferred_element_type=F32)


def span_of(index, size):
    return pl.ds(pl.multiple_of(index * size, size), size)


def store_pairs(values, weight, points, pairs, span):
    phi = values[: NI * points].astype(F32) * weight
    psi = values[NI * points :].astype(F32)
    for i in range(NI):
        for k in range(NC):
            product = phi[i * points : (i + 1) * points] * psi[k * points : (k + 1) * points]
            row = (i * NC + k) * points
            pairs[row : row + points, span] = product.astype(BF16)


def angular_density(step, x, values_of, store, table, weight, degree_ref, part_ref, ends_at, pairs, work):
    half = part_ref.shape[0] // NC
    points = 2 * half
    steps = table.shape[0] // CHUNK

    def angular(i, carry):
        span = span_of(i, CHUNK)
        phi, psi = values_of(i, span)
        low_high = phi.reshape(2, half, CHUNK)
        store(span, jnp.where(x == 0, low_high[0], low_high[1]), psi)
        phi = phi.astype(F32) * weight[:, span]
        psi = psi.astype(F32)
        for k in range(NC):
            rows = slice(k * points, (k + 1) * points)
            pairs[rows, span] = (phi * psi[rows]).astype(BF16)
        return carry

    lax.fori_loop(0, steps, angular, 0)

    def density(t, carry):
        span = span_of(t, TILE)
        degree = degree_ref[:, span]
        work[...] = dot_nn(pairs[...], table[:, span])
        position = lax.broadcasted_iota(jnp.int32, (half, TILE), 0).astype(F32)
        ahead = jnp.exp((degree + 1.0) * step * (position - (half - 1.0)))
        behind = jnp.exp(-degree * step * position)
        for k in range(NC):
            low = work[k * points : k * points + half, :]
            high = work[k * points + half : (k + 1) * points, :]
            part_ref[k * half : (k + 1) * half, span] = jnp.where(x == 0, low, high).astype(BF16)
            ends = (low * ahead, high * ahead, low * behind, high * behind)
            for n in range(4):
                ends_at(n, k, span, jnp.sum(ends[n], axis=0, keepdims=True))
        return carry

    lax.fori_loop(0, table.shape[1] // TILE, density, 0)


def own_kernel(
    step, place, own, cont, weight, degree_ref, table_hbm,
    part_any, phi_any, psi_ref, ends_ref, table,
    part_ref, phi_ref, rows, pairs, work, sems,
):
    points = own.shape[0]
    steps = table.shape[0] // CHUNK

    def fetch(i):
        return pltpu.make_async_copy(
            table_hbm.at[span_of(i, CHUNK)], table.at[span_of(i, CHUNK)], sems.at[i]
        )

    for i in range(steps):
        fetch(i).start()
    rows[:points, :] = own[...]
    rows[points:, :] = cont[...]

    def values_of(i, span):
        fetch(i).wait()
        values = dot_nt(rows[...], table[span, :]).astype(BF16)
        return values[:points], values[points:]

    def store(span, phi, psi):
        phi_ref[:, span] = phi
        psi_ref[:, span] = psi

    def ends_at(n, k, span, value):
        ends_ref[n * NC + k : n * NC + k + 1, span] = value

    angular_density(
        step, place[0], values_of, store, table, weight, degree_ref, part_ref, ends_at, pairs, work
    )
    copies = [
        pltpu.make_async_copy(part_ref, part_any, sems.at[0]),
        pltpu.make_async_copy(phi_ref, phi_any, sems.at[1]),
    ]
    for copy in copies:
        copy.start()
    for copy in copies:
        copy.wait()


def other_kernel(
    step, place, other, psi_ref, weight, degree_ref, own_ends, table,
    part_any, phi_any, ends_ref,
    part_ref, phi_ref, pairs, work, sems,
):
    x = place[0]

    def values_of(i, span):
        return dot_nt(other[...], table[span, :]).astype(BF16), psi_ref[:, span]

    def store(span, phi, psi):
        phi_ref[:, span] = phi

    def ends_at(n, k, span, value):
        ends_ref[pl.ds(n * NP + (1 - x) * NC + k, 1), span] = value

    for n in range(4):
        for k in range(NC):
            ends_ref[pl.ds(n * NP + x * NC + k, 1), :] = own_ends[n * NC + k : n * NC + k + 1, :]
    angular_density(
        step, x, values_of, store, table, weight, degree_ref, part_ref, ends_at, pairs, work
    )
    copies = [
        pltpu.make_async_copy(part_ref, part_any, sems.at[0]),
        pltpu.make_async_copy(phi_ref, phi_any, sems.at[1]),
    ]
    for copy in copies:
        copy.start()
    for copy in copies:
        copy.wait()


def finish_kernel(
    step, pieces, place, own, other, cont, weight, degree_ref, earlier, later, arrived,
    part_any, other_part_any, phi_any, other_phi_any, table_hbm, *refs
):
    far_hbm = refs[:pieces]
    send_any, keep_any, far_weight, send_ref, keep_ref, part, table, far_table, rows, pairs, sorted_pairs, phi_all, pot, product, work, total, sems = refs[pieces:]
    x = place[0]
    points = own.shape[0]
    half = points // 2
    quad, channels = table.shape
    steps = quad // WIDE

    def fetch_far(n):
        size = far_hbm[n].shape[0]
        start = pl.multiple_of(place[1 + n], quad // 16)
        return pltpu.make_async_copy(far_hbm[n], far_table.at[pl.ds(start, size)], sems.at[n])

    def fetch_rows():
        near = span_of(x, half)
        yield pltpu.make_async_copy(own.at[near], rows.at[near], sems.at[pieces])
        for k in range(NC):
            at = span_of(2 * k + x, half)
            to = pl.ds((NI + k) * half, half)
            yield pltpu.make_async_copy(cont.at[at], rows.at[to], sems.at[pieces + 1 + k])

    fetch_table = pltpu.make_async_copy(table_hbm, table, sems.at[pieces + 1 + NC])
    for copy in fetch_rows():
        copy.start()

    for n in range(pieces):
        fetch_far(n).start()
    near = [
        pltpu.make_async_copy(phi_any, phi_all.at[span_of(x, half), pl.ds(0, quad)], sems.at[pieces + 2 + NC]),
        pltpu.make_async_copy(other_phi_any, phi_all.at[span_of(1 - x, half), pl.ds(0, quad)], sems.at[pieces + 3 + NC]),
        pltpu.make_async_copy(part_any, part.at[span_of(x, NC * half)], sems.at[pieces + 4 + NC]),
        pltpu.make_async_copy(other_part_any, part.at[span_of(1 - x, NC * half)], sems.at[pieces + 5 + NC]),
    ]
    for copy in near:
        copy.start()
    fetch_table.start()
    rows[span_of(1 - x, half), :] = other[span_of(x, half), :]
    far_weight[...] = jnp.zeros_like(far_weight)
    for row in (2 * NP + 2, 2 * NP + 1, 2 * NP):
        far_weight[...] += arrived[row : row + 1, :quad].astype(F32)
    for copy in fetch_rows():
        copy.wait()
    for n in range(pieces):
        fetch_far(n).wait()

    shape = (NP * half, NP * half)
    row, column = (lax.broadcasted_iota(jnp.int32, shape, n) for n in range(2))
    by_point = ((row & (NP - 1)) * half + (row >> 3) == column).astype(F32).astype(BF16)
    by_pair = ((column & (NP - 1)) * half + (column >> 3) == row).astype(F32).astype(BF16)

    def angular(i, carry):
        span = span_of(i, WIDE)
        values = dot_nt(rows[...], far_table[span, :]).astype(BF16)
        store_pairs(values, far_weight[:, span], half, pairs, span)
        phi_all[:, span_of(i + steps, WIDE)] = values[: NI * half]
        sorted_pairs[:, span] = dot_nn(by_point, pairs[:, span]).astype(BF16)
        return carry

    lax.fori_loop(0, steps, angular, 0)
    for copy in near:
        copy.wait()

    def radial(t, carry):
        span = span_of(t, TILE)
        degree = degree_ref[:, span]
        shrink_ahead = jnp.exp(-(degree + 1.0) * step)
        shrink_behind = jnp.exp(-degree * step)
        factor = 4.0 * step / (2.0 * degree + 1.0)
        density = dot_nn(sorted_pairs[...], far_table[:, span]) + dot_nn(by_point, part[:, span])
        work[...] = density.reshape(half, NP, TILE)
        came = arrived[:, span].astype(F32)
        ahead = earlier[:, span] + came[:NP]
        behind = (later[:, span] + came[NP : 2 * NP]) * shrink_behind
        for j in range(half):
            ahead = ahead * shrink_ahead + work[j]
            total[j] = ahead
        for j in range(half - 1, -1, -1):
            total[j] = factor * (total[j] + behind)
            behind = (behind + work[j]) * shrink_behind
        potential = total[...].reshape(NP * half, TILE).astype(BF16)
        pot[:, span] = dot_nn(by_pair, potential).astype(BF16)
        return carry

    lax.fori_loop(0, channels // TILE, radial, 0)

    def weigh(source, weight_at, first):
        def chunk(i, carry):
            span = span_of(i, WIDE)
            at = span_of(i + first, WIDE)
            angle = dot_nt(pot[...], source[span, :])
            values = phi_all[:, at].astype(F32) * weight_at[:, span]
            for k in range(NC):
                value = jnp.zeros((half, WIDE), F32)
                for o in range(NI):
                    row = (o * NC + k) * half
                    value += values[o * half : (o + 1) * half] * angle[row : row + half]
                product[k * half : (k + 1) * half, at] = value.astype(BF16)
            return carry

        lax.fori_loop(0, steps, chunk, 0)

    weigh(far_table, far_weight, steps)
    fetch_table.wait()
    weigh(table, weight, 0)
    share = channels // 2
    leave = []
    for n, (out, to, first) in enumerate(
        ((send_ref, send_any, (1 - x) * share), (keep_ref, keep_any, x * share))
    ):
        at = pl.ds(pl.multiple_of(first, share), share)
        value = dot_nn(product[:, :quad], table[:, at]) + dot_nn(product[:, quad:], far_table[:, at])
        out[...] = (-value).astype(out.dtype)
        leave.append(pltpu.make_async_copy(out, to, sems.at[n]))
        leave[n].start()
    for copy in leave:
        copy.wait()


def slab_kernel(place, table, *refs):
    sems = refs[-1]
    copies = []
    for n, out in enumerate(refs[:-1]):
        start = pl.multiple_of(place[n], 80)
        copies.append(pltpu.make_async_copy(table.at[pl.ds(start, out.shape[0])], out, sems.at[n]))
    for copy in copies:
        copy.start()
    for copy in copies:
        copy.wait()


def place_kernel(place, keep, came, out_ref):
    x = place[0]
    half = keep.shape[0] // NC
    out_ref[:, span_of(x, half), :] = keep[...].reshape(NC, half, -1)
    out_ref[:, span_of(1 - x, half), :] = came[...].astype(F32).reshape(NC, half, -1)


VMEM_SPEC = pl.BlockSpec(memory_space=pltpu.VMEM)
SMEM_SPEC = pl.BlockSpec(memory_space=pltpu.SMEM)
HBM_SPEC = pl.BlockSpec(memory_space=pl.ANY)
ANY_SPEC = HBM_SPEC


def shards_by_table(orbitals, continuum, harmonic_table, ang_weight, channel_lm):
    quad, channels = harmonic_table.shape
    points = orbitals.shape[1]
    half = points // 2
    step = LOG_SPAN / (points * lax.axis_size("grid"))
    x = lax.axis_index("orb")
    g = lax.axis_index("grid")
    core, y, z = g % 2, (g // 2) % 2, g // 4
    across = [(0, 1), (1, 0)]
    everyone = range(16)

    def over_x(value):
        return lax.ppermute(value, "orb", across)

    def flip(value, bits):
        return lax.ppermute(value, "grid", [(n, n ^ bits) for n in everyone])

    pieces = 14
    size = quad // 16
    corner = 2 * (z % 2) + y

    def offset(which, side, n):
        return ((which * 2 + side) * 2 + n) * size

    def after(value, *others):
        return lax.optimization_barrier((value, *others))[0]

    def in_hbm(value):
        return pltpu.with_memory_space_constraint(value, pltpu.HBM)

    hbm = pl.BlockSpec(memory_space=pltpu.HBM)
    slabs = pl.pallas_call(
        slab_kernel,
        out_shape=tuple(jax.ShapeDtypeStruct((n * size, channels), BF16) for n in (1, 1, 2)),
        in_specs=[SMEM_SPEC, hbm],
        out_specs=(VMEM_SPEC,) * 3,
        scratch_shapes=[pltpu.SemaphoreType.DMA((3,))],
        name="slabs",
    )(
        jnp.stack([offset(corner, core, 0), offset(corner, core, 1), offset(corner ^ 3, core, 0)]),
        in_hbm(harmonic_table),
    )

    own = orbitals[0]
    weight = ang_weight[None, :]
    degree = channel_degree(channel_lm)[None, :]
    cont = continuum.reshape(NC * points, channels)
    place = jnp.stack([x, offset(corner, core, 1)]).astype(jnp.int32)
    part_shape = jax.ShapeDtypeStruct((NC * half, channels), BF16)
    phi_shape = jax.ShapeDtypeStruct((half, quad), BF16)

    other = over_x(own)
    first_a = over_x(slabs[0])
    first_b = over_x(slabs[1])
    last = over_x(slabs[2])
    part, phi, psi, own_ends, table = pl.pallas_call(
        functools.partial(own_kernel, step),
        out_shape=(
            part_shape,
            phi_shape,
            jax.ShapeDtypeStruct((NC * points, quad), BF16),
            jax.ShapeDtypeStruct((4 * NC, channels), F32),
            jax.ShapeDtypeStruct((quad, channels), BF16),
        ),
        in_specs=[SMEM_SPEC] + [VMEM_SPEC] * 4 + [pl.BlockSpec(memory_space=pltpu.HBM)],
        out_specs=(ANY_SPEC,) * 2 + (VMEM_SPEC,) * 3,
        scratch_shapes=[
            pltpu.VMEM((NC * half, channels), BF16),
            pltpu.VMEM((half, quad), BF16),
            pltpu.VMEM(((1 + NC) * points, channels), BF16),
            pltpu.VMEM((NC * points, quad), BF16),
            pltpu.VMEM((NC * points, TILE), F32),
            pltpu.SemaphoreType.DMA((quad // CHUNK,)),
        ],
        compiler_params=pltpu.CompilerParams(vmem_limit_bytes=16 << 20),
        name="own_orbital",
    )(place, own, cont, weight, degree, in_hbm(after(harmonic_table, slabs[0])))
    other_part, other_phi, ends = pl.pallas_call(
        functools.partial(other_kernel, step),
        out_shape=(
            part_shape,
            phi_shape,
            jax.ShapeDtypeStruct((4 * NP, channels), F32),
        ),
        in_specs=[SMEM_SPEC] + [VMEM_SPEC] * 6,
        out_specs=(ANY_SPEC, ANY_SPEC, VMEM_SPEC),
        scratch_shapes=[
            pltpu.VMEM((NC * half, channels), BF16),
            pltpu.VMEM((half, quad), BF16),
            pltpu.VMEM((NC * points, quad), BF16),
            pltpu.VMEM((NC * points, TILE), F32),
            pltpu.SemaphoreType.DMA((3,)),
        ],
        compiler_params=pltpu.CompilerParams(vmem_limit_bytes=8 << 20),
        name="other_orbital",
    )(place, other, psi, weight, degree, own_ends, table)
    ends = ends.reshape(4, NP, channels)
    ahead_rate = (degree + 1.0) * step
    behind_rate = degree * step

    def ahead_by(count):
        return jnp.exp(-ahead_rate * count)

    def behind_by(count):
        return jnp.exp(-behind_rate * count)

    low_end, high_end, low_start, high_start = ends[0], ends[1], ends[2], ends[3]
    block_end = high_end + ahead_by(half) * low_end
    block_start = low_start + behind_by(half) * high_start
    u = g % 4
    both = jnp.concatenate([block_end, block_start], axis=0)
    message = both.astype(BF16)
    first_a = after(first_a, message)
    by_y_a, by_z_a = flip(first_a, 2), flip(first_a, 4)
    earlier = jnp.zeros((NP, channels), F32)
    later = jnp.zeros((NP, channels), F32)
    row_end = ahead_by(points * (3 - u)) * block_end
    row_start = behind_by(points * u) * block_start
    for bits in (1, 2, 3):
        came = flip(message, bits).astype(F32)
        v = u ^ bits
        distance = jnp.abs(u - v) - 1
        before = v < u
        earlier += jnp.where(before, ahead_by(points * distance), 0.0) * came[:NP]
        later += jnp.where(before, 0.0, behind_by(points * distance)) * came[NP:]
        row_end += ahead_by(points * (3 - v)) * came[:NP]
        row_start += behind_by(points * v) * came[NP:]
    row_end = after(row_end.astype(BF16), first_a, first_b)
    row_start = after(row_start.astype(BF16), first_a, first_b)
    for shift in (1, 2, 3):
        message = jnp.where(z + shift < 4, row_end, row_start)
        came = lax.ppermute(message, "grid", [(n, (n + 4 * shift) % 16) for n in everyone])
        came = after(came, by_y_a, by_z_a, last)
        came = came.astype(F32)
        source = (z - shift) % 4
        before = source < z
        distance = jnp.abs(z - source) - 1
        earlier += jnp.where(before, ahead_by(points * (4 * distance + u)), 0.0) * came
        later += jnp.where(before, 0.0, behind_by(points * (4 * distance + 3 - u))) * came
    upper_earlier = low_end + ahead_by(half) * earlier
    lower_later = high_start + behind_by(half) * later
    theirs = jnp.concatenate(
        [jnp.where(x == 0, upper_earlier, earlier), jnp.where(x == 0, later, lower_later)], axis=0
    )
    terms, rest = [], weight
    for _ in range(3):
        terms.append(lax.reduce_precision(rest, 8, 7))
        rest = rest - terms[-1]
    terms = jnp.pad(jnp.concatenate(terms, axis=0), ((0, NP - 3), (0, channels - quad)))
    theirs = jnp.concatenate([theirs, terms], axis=0)
    theirs = theirs.astype(BF16)
    arrived = over_x(theirs)
    earlier = jnp.where(x == 0, earlier, upper_earlier)
    later = jnp.where(x == 0, lower_later, later)
    first_b = after(first_b, row_end)
    received = [first_a, first_b, last]
    received += [by_y_a, by_z_a, flip(first_b, 2), flip(first_b, 4)]
    which = [(corner, 0), (corner, 1), (corner ^ 3, 0)]
    which += [(corner ^ 1, 0), (corner ^ 2, 0), (corner ^ 1, 1), (corner ^ 2, 1)]
    far = received + [flip(value, 1) for value in received]
    offsets = [offset(w, core, n) for w, n in which] + [offset(w, 1 - core, n) for w, n in which]
    places = jnp.stack([x] + offsets).astype(jnp.int32)

    send, keep = pl.pallas_call(
        functools.partial(finish_kernel, step, pieces),
        out_shape=(
            jax.ShapeDtypeStruct((NC * half, channels // 2), BF16),
            jax.ShapeDtypeStruct((NC * half, channels // 2), F32),
        ),
        in_specs=[SMEM_SPEC, hbm, VMEM_SPEC, hbm] + [VMEM_SPEC] * 5 + [hbm] * 5 + [ANY_SPEC] * pieces,
        out_specs=(ANY_SPEC,) * 2,
        scratch_shapes=[
            pltpu.VMEM((1, quad), F32),
            pltpu.VMEM((NC * half, channels // 2), BF16),
            pltpu.VMEM((NC * half, channels // 2), F32),
            pltpu.VMEM((NP * half, channels), BF16),
            pltpu.VMEM((quad, channels), BF16),
            pltpu.VMEM((quad, channels), BF16),
            pltpu.VMEM(((NI + NC) * half, channels), BF16),
            pltpu.VMEM((NP * half, quad), BF16),
            pltpu.VMEM((NP * half, quad), BF16),
            pltpu.VMEM((NI * half, 2 * quad), BF16),
            pltpu.VMEM((NP * half, channels), BF16),
            pltpu.VMEM((NC * half, 2 * quad), BF16),
            pltpu.VMEM((half, NP, TILE), F32),
            pltpu.VMEM((half, NP, TILE), F32),
            pltpu.SemaphoreType.DMA((pieces + 6 + NC,)),
        ],
        compiler_params=pltpu.CompilerParams(vmem_limit_bytes=30 << 20),
        name="finish",
    )(
        places, in_hbm(own), other, in_hbm(cont), weight, degree, earlier, later, arrived,
        in_hbm(part), in_hbm(other_part), in_hbm(phi), in_hbm(other_phi), in_hbm(harmonic_table), *far,
    )
    came = over_x(send)
    out = pl.pallas_call(
        place_kernel,
        out_shape=jax.ShapeDtypeStruct((NC, points, channels // 2), F32),
        in_specs=[SMEM_SPEC, VMEM_SPEC, VMEM_SPEC],
        out_specs=VMEM_SPEC,
        name="place",
    )(place, keep, came)
    return jnp.transpose(out, (2, 0, 1))


def solution(mesh):
    small = dict(mesh.shape) == {"orb": 2, "grid": 16}
    return jax.shard_map(
        shards_by_table if small else shards,
        mesh=mesh,
        in_specs=(P("orb", "grid", None), P(None, "grid", None), P("orb", None), P("orb"), P()),
        out_specs=P("orb", None, "grid"),
        check_vma=False,
    )
```

```python
import functools
import math

import jax
import jax.numpy as jnp
from jax import lax
from jax.experimental import pallas as pl
from jax.experimental.pallas import tpu as pltpu
from jax.sharding import PartitionSpec as P

LMAX = 47
LM = 2304


LOG_SPAN = 7.0


def combine(earlier, later):
    return (earlier[0] * later[0], earlier[1] * later[0] + later[1])


def channel_degree(lm_index):
    levels = jnp.arange(1, LMAX + 1, dtype=jnp.int32)
    return jnp.sum((lm_index[:, None] >= levels * levels).astype(jnp.float32), axis=1)


def line_sums(forward_source, backward_source, decay_rate, block_size):
    lead_first, lead_second, count, channels = forward_source.shape
    block_count = count // block_size
    forward_blocks = forward_source.reshape(
        lead_first, lead_second, block_count, block_size, channels
    )
    backward_blocks = backward_source.reshape(
        lead_first, lead_second, block_count, block_size, channels
    )
    forward = forward_blocks
    backward = backward_blocks
    for distance in range(1, block_size):
        factor = jnp.exp(-decay_rate * distance)
        padding = jnp.zeros((lead_first, lead_second, block_count, distance, channels), jnp.float32)
        forward = forward + factor * jnp.concatenate(
            [padding, forward_blocks[:, :, :, : block_size - distance]], axis=3
        )
        backward = backward + factor * jnp.concatenate(
            [backward_blocks[:, :, :, distance:], padding], axis=3
        )
    block_decay = jnp.broadcast_to(
        jnp.exp(-decay_rate * block_size), (lead_first, lead_second, block_count, channels)
    )
    forward_total = lax.associative_scan(
        combine, (block_decay, forward[:, :, :, block_size - 1]), axis=2
    )[1]
    backward_total = lax.associative_scan(
        combine, (block_decay, backward[:, :, :, 0]), reverse=True, axis=2
    )[1]
    boundary = jnp.zeros((lead_first, lead_second, 1, channels), jnp.float32)
    earlier_sum = jnp.concatenate([boundary, forward_total[:, :, : block_count - 1]], axis=2)
    later_sum = jnp.concatenate([backward_total[:, :, 1:], boundary], axis=2)
    offsets = jnp.arange(block_size, dtype=jnp.float32)[:, None]
    forward = forward + jnp.exp(-decay_rate * (offsets + 1.0)) * earlier_sum[:, :, :, None, :]
    backward = (
        backward + jnp.exp(-decay_rate * (block_size - offsets)) * later_sum[:, :, :, None, :]
    )
    shape = forward_source.shape
    return (
        forward.reshape(shape),
        backward.reshape(shape),
        forward_total[:, :, block_count - 1],
        backward_total[:, :, 0],
    )


def local_lines(density, degree, points):
    count = density.shape[2]
    increment = LOG_SPAN / points
    positions = jnp.arange(count, dtype=jnp.int32).astype(jnp.float32)[:, None]
    radius = jnp.exp((positions + 1.0 - points) * increment)
    decay_rate = degree * increment
    source = increment * radius * density
    scaled = increment * density
    forward, backward, forward_end, backward_end = line_sums(
        source, scaled, decay_rate, math.gcd(count, 16)
    )
    return (forward, backward, forward_end, backward_end, radius, scaled, decay_rate)


def finish_potential(forward, backward, radius, scaled, degree):
    factor = 4.0 / (2.0 * degree + 1.0)
    return factor * (forward / radius + backward - scaled)


def shards(orbitals, continuum, harmonic_table, ang_weight, channel_lm):
    analysis = (ang_weight[:, None] * harmonic_table.astype(jnp.float32)).astype(jnp.bfloat16)
    phi_ang = jnp.einsum(
        "al,irl->ira",
        harmonic_table,
        lax.all_gather(orbitals, "orb", axis=0, tiled=True),
        preferred_element_type=jnp.float32,
    ).astype(jnp.bfloat16)
    continuum_angular = jnp.einsum(
        "al,krl->kra", harmonic_table, continuum, preferred_element_type=jnp.float32
    ).astype(jnp.bfloat16)
    pair_values = (
        phi_ang.astype(jnp.float32)[:, None] * continuum_angular.astype(jnp.float32)[None]
    ).astype(jnp.bfloat16)
    density = lax.psum_scatter(
        jnp.einsum(
            "al,ikra->ikrl", analysis, pair_values, preferred_element_type=jnp.float32
        ).astype(jnp.bfloat16),
        "orb",
        scatter_dimension=0,
        tiled=True,
    )
    local_count = LM // lax.axis_size("grid")
    local_channel_index = lax.dynamic_slice_in_dim(
        channel_lm, lax.axis_index("grid") * local_count, local_count
    )
    degree = channel_degree(local_channel_index)
    line_density = lax.all_to_all(density, "grid", split_axis=3, concat_axis=2, tiled=True)
    points = line_density.shape[2]
    forward, backward, forward_end, backward_end, radius, scaled, decay_rate = local_lines(
        line_density.astype(jnp.float32), degree, points
    )
    potential = finish_potential(forward, backward, radius, scaled, degree).astype(jnp.bfloat16)
    radial_potential = lax.all_to_all(potential, "grid", split_axis=2, concat_axis=3, tiled=True)
    pot_ang = jnp.einsum(
        "al,ikrl->ikra",
        harmonic_table,
        lax.all_gather(radial_potential, "orb", axis=0, tiled=True),
        preferred_element_type=jnp.float32,
    )
    weighted_values = jnp.sum(phi_ang.astype(jnp.float32)[:, None] * pot_ang, axis=0)
    product = weighted_values.astype(jnp.bfloat16)
    return -lax.psum_scatter(
        jnp.einsum("al,kra->lkr", analysis, product, preferred_element_type=jnp.float32),
        "orb",
        scatter_dimension=0,
        tiled=True,
    )


NC = 4
NI = 2
NP = NI * NC
CHUNK = 256
WIDE = 640
TILE = 768
F32 = jnp.float32
BF16 = jnp.bfloat16


def dot_nt(a, b):
    return lax.dot_general(a, b, (((1,), (1,)), ((), ())), preferred_element_type=F32)


def dot_nn(a, b):
    return jnp.dot(a, b, preferred_element_type=F32)


def span_of(index, size):
    return pl.ds(pl.multiple_of(index * size, size), size)


def store_pairs(values, weight, points, pairs, span):
    phi = values[: NI * points].astype(F32) * weight
    psi = values[NI * points :].astype(F32)
    for i in range(NI):
        for k in range(NC):
            product = phi[i * points : (i + 1) * points] * psi[k * points : (k + 1) * points]
            row = (i * NC + k) * points
            pairs[row : row + points, span] = product.astype(BF16)


def angular_density(step, x, values_of, store, table, weight, degree_ref, part_ref, ends_at, pairs, work):
    half = part_ref.shape[0] // NC
    points = 2 * half
    steps = table.shape[0] // CHUNK

    def angular(i, carry):
        span = span_of(i, CHUNK)
        phi, psi = values_of(i, span)
        low_high = phi.reshape(2, half, CHUNK)
        store(span, jnp.where(x == 0, low_high[0], low_high[1]), psi)
        phi = phi.astype(F32) * weight[:, span]
        psi = psi.astype(F32)
        for k in range(NC):
            rows = slice(k * points, (k + 1) * points)
            pairs[rows, span] = (phi * psi[rows]).astype(BF16)
        return carry

    lax.fori_loop(0, steps, angular, 0)

    def density(t, carry):
        span = span_of(t, TILE)
        degree = degree_ref[:, span]
        work[...] = dot_nn(pairs[...], table[:, span])
        position = lax.broadcasted_iota(jnp.int32, (half, TILE), 0).astype(F32)
        ahead = jnp.exp((degree + 1.0) * step * (position - (half - 1.0)))
        behind = jnp.exp(-degree * step * position)
        for k in range(NC):
            low = work[k * points : k * points + half, :]
            high = work[k * points + half : (k + 1) * points, :]
            part_ref[k * half : (k + 1) * half, span] = jnp.where(x == 0, low, high).astype(BF16)
            ends = (low * ahead, high * ahead, low * behind, high * behind)
            for n in range(4):
                ends_at(n, k, span, jnp.sum(ends[n], axis=0, keepdims=True))
        return carry

    lax.fori_loop(0, table.shape[1] // TILE, density, 0)


def own_kernel(
    step, place, own, cont, weight, degree_ref, table_hbm,
    part_any, phi_any, psi_ref, ends_ref, table,
    part_ref, phi_ref, rows, pairs, work, sems,
):
    points = own.shape[0]
    steps = table.shape[0] // CHUNK

    def fetch(i):
        return pltpu.make_async_copy(
            table_hbm.at[span_of(i, CHUNK)], table.at[span_of(i, CHUNK)], sems.at[i]
        )

    for i in range(steps):
        fetch(i).start()
    rows[:points, :] = own[...]
    rows[points:, :] = cont[...]

    def values_of(i, span):
        fetch(i).wait()
        values = dot_nt(rows[...], table[span, :]).astype(BF16)
        return values[:points], values[points:]

    def store(span, phi, psi):
        phi_ref[:, span] = phi
        psi_ref[:, span] = psi

    def ends_at(n, k, span, value):
        ends_ref[n * NC + k : n * NC + k + 1, span] = value

    angular_density(
        step, place[0], values_of, store, table, weight, degree_ref, part_ref, ends_at, pairs, work
    )
    copies = [
        pltpu.make_async_copy(part_ref, part_any, sems.at[0]),
        pltpu.make_async_copy(phi_ref, phi_any, sems.at[1]),
    ]
    for copy in copies:
        copy.start()
    for copy in copies:
        copy.wait()


def other_kernel(
    step, place, other, psi_ref, weight, degree_ref, own_ends, table,
    part_any, phi_any, ends_ref,
    part_ref, phi_ref, pairs, work, sems,
):
    x = place[0]

    def values_of(i, span):
        return dot_nt(other[...], table[span, :]).astype(BF16), psi_ref[:, span]

    def store(span, phi, psi):
        phi_ref[:, span] = phi

    def ends_at(n, k, span, value):
        ends_ref[pl.ds(n * NP + (1 - x) * NC + k, 1), span] = value

    for n in range(4):
        for k in range(NC):
            ends_ref[pl.ds(n * NP + x * NC + k, 1), :] = own_ends[n * NC + k : n * NC + k + 1, :]
    angular_density(
        step, x, values_of, store, table, weight, degree_ref, part_ref, ends_at, pairs, work
    )
    copies = [
        pltpu.make_async_copy(part_ref, part_any, sems.at[0]),
        pltpu.make_async_copy(phi_ref, phi_any, sems.at[1]),
    ]
    for copy in copies:
        copy.start()
    for copy in copies:
        copy.wait()


def finish_kernel(
    step, pieces, place, own, other, cont, weight, degree_ref, earlier, later, arrived,
    part_any, other_part_any, phi_any, other_phi_any, table_hbm, *refs
):
    far_hbm = refs[:pieces]
    send_any, keep_any, far_weight, send_ref, keep_ref, part, table, far_table, rows, pairs, sorted_pairs, phi_all, pot, product, work, total, sems = refs[pieces:]
    x = place[0]
    points = own.shape[0]
    half = points // 2
    quad, channels = table.shape
    steps = quad // WIDE

    def fetch_far(n):
        size = far_hbm[n].shape[0]
        start = pl.multiple_of(place[1 + n], quad // 16)
        return pltpu.make_async_copy(far_hbm[n], far_table.at[pl.ds(start, size)], sems.at[n])

    def fetch_rows():
        near = span_of(x, half)
        yield pltpu.make_async_copy(own.at[near], rows.at[near], sems.at[pieces])
        for k in range(NC):
            at = span_of(2 * k + x, half)
            to = pl.ds((NI + k) * half, half)
            yield pltpu.make_async_copy(cont.at[at], rows.at[to], sems.at[pieces + 1 + k])

    fetch_table = pltpu.make_async_copy(table_hbm, table, sems.at[pieces + 1 + NC])
    for copy in fetch_rows():
        copy.start()

    for n in range(pieces):
        fetch_far(n).start()
    near = [
        pltpu.make_async_copy(phi_any, phi_all.at[span_of(x, half), pl.ds(0, quad)], sems.at[pieces + 2 + NC]),
        pltpu.make_async_copy(other_phi_any, phi_all.at[span_of(1 - x, half), pl.ds(0, quad)], sems.at[pieces + 3 + NC]),
        pltpu.make_async_copy(part_any, part.at[span_of(x, NC * half)], sems.at[pieces + 4 + NC]),
        pltpu.make_async_copy(other_part_any, part.at[span_of(1 - x, NC * half)], sems.at[pieces + 5 + NC]),
    ]
    for copy in near:
        copy.start()
    fetch_table.start()
    rows[span_of(1 - x, half), :] = other[span_of(x, half), :]
    far_weight[...] = jnp.zeros_like(far_weight)
    for row in (2 * NP + 2, 2 * NP + 1, 2 * NP):
        far_weight[...] += arrived[row : row + 1, :quad].astype(F32)
    for copy in fetch_rows():
        copy.wait()
    for n in range(pieces):
        fetch_far(n).wait()

    shape = (NP * half, NP * half)
    row, column = (lax.broadcasted_iota(jnp.int32, shape, n) for n in range(2))
    by_point = ((row & (NP - 1)) * half + (row >> 3) == column).astype(F32).astype(BF16)
    by_pair = ((column & (NP - 1)) * half + (column >> 3) == row).astype(F32).astype(BF16)

    def angular(i, carry):
        span = span_of(i, WIDE)
        values = dot_nt(rows[...], far_table[span, :]).astype(BF16)
        store_pairs(values, far_weight[:, span], half, pairs, span)
        phi_all[:, span_of(i + steps, WIDE)] = values[: NI * half]
        sorted_pairs[:, span] = dot_nn(by_point, pairs[:, span]).astype(BF16)
        return carry

    lax.fori_loop(0, steps, angular, 0)
    for copy in near:
        copy.wait()

    def radial(t, carry):
        span = span_of(t, TILE)
        degree = degree_ref[:, span]
        shrink_ahead = jnp.exp(-(degree + 1.0) * step)
        shrink_behind = jnp.exp(-degree * step)
        factor = 4.0 * step / (2.0 * degree + 1.0)
        density = dot_nn(sorted_pairs[...], far_table[:, span]) + dot_nn(by_point, part[:, span])
        work[...] = density.reshape(half, NP, TILE)
        came = arrived[:, span].astype(F32)
        ahead = earlier[:, span] + came[:NP]
        behind = (later[:, span] + came[NP : 2 * NP]) * shrink_behind
        for j in range(half):
            ahead = ahead * shrink_ahead + work[j]
            total[j] = ahead
        for j in range(half - 1, -1, -1):
            total[j] = factor * (total[j] + behind)
            behind = (behind + work[j]) * shrink_behind
        potential = total[...].reshape(NP * half, TILE).astype(BF16)
        pot[:, span] = dot_nn(by_pair, potential).astype(BF16)
        return carry

    lax.fori_loop(0, channels // TILE, radial, 0)

    def weigh(source, weight_at, first):
        def chunk(i, carry):
            span = span_of(i, WIDE)
            at = span_of(i + first, WIDE)
            angle = dot_nt(pot[...], source[span, :])
            values = phi_all[:, at].astype(F32) * weight_at[:, span]
            for k in range(NC):
                value = jnp.zeros((half, WIDE), F32)
                for o in range(NI):
                    row = (o * NC + k) * half
                    value += values[o * half : (o + 1) * half] * angle[row : row + half]
                product[k * half : (k + 1) * half, at] = value.astype(BF16)
            return carry

        lax.fori_loop(0, steps, chunk, 0)

    weigh(far_table, far_weight, steps)
    fetch_table.wait()
    weigh(table, weight, 0)
    share = channels // 2
    leave = []
    for n, (out, to, first) in enumerate(
        ((send_ref, send_any, (1 - x) * share), (keep_ref, keep_any, x * share))
    ):
        at = pl.ds(pl.multiple_of(first, share), share)
        value = dot_nn(product[:, :quad], table[:, at]) + dot_nn(product[:, quad:], far_table[:, at])
        out[...] = (-value).astype(out.dtype)
        leave.append(pltpu.make_async_copy(out, to, sems.at[n]))
        leave[n].start()
    for copy in leave:
        copy.wait()


def slab_kernel(place, table, *refs):
    sems = refs[-1]
    copies = []
    for n, out in enumerate(refs[:-1]):
        start = pl.multiple_of(place[n], 80)
        copies.append(pltpu.make_async_copy(table.at[pl.ds(start, out.shape[0])], out, sems.at[n]))
    for copy in copies:
        copy.start()
    for copy in copies:
        copy.wait()


def place_kernel(place, keep, came, out_ref):
    x = place[0]
    half = keep.shape[0] // NC
    out_ref[:, span_of(x, half), :] = keep[...].reshape(NC, half, -1)
    out_ref[:, span_of(1 - x, half), :] = came[...].astype(F32).reshape(NC, half, -1)


VMEM_SPEC = pl.BlockSpec(memory_space=pltpu.VMEM)
SMEM_SPEC = pl.BlockSpec(memory_space=pltpu.SMEM)
HBM_SPEC = pl.BlockSpec(memory_space=pl.ANY)
ANY_SPEC = HBM_SPEC


def shards_by_table(orbitals, continuum, harmonic_table, ang_weight, channel_lm):
    quad, channels = harmonic_table.shape
    points = orbitals.shape[1]
    half = points // 2
    step = LOG_SPAN / (points * lax.axis_size("grid"))
    x = lax.axis_index("orb")
    g = lax.axis_index("grid")
    core, y, z = g % 2, (g // 2) % 2, g // 4
    across = [(0, 1), (1, 0)]
    everyone = range(16)

    def over_x(value):
        return lax.ppermute(value, "orb", across)

    def flip(value, bits):
        return lax.ppermute(value, "grid", [(n, n ^ bits) for n in everyone])

    pieces = 14
    size = quad // 16
    corner = 2 * (z % 2) + y

    def offset(which, side, n):
        return ((which * 2 + side) * 2 + n) * size

    def after(value, *others):
        return lax.optimization_barrier((value, *others))[0]

    def in_hbm(value):
        return pltpu.with_memory_space_constraint(value, pltpu.HBM)

    hbm = pl.BlockSpec(memory_space=pltpu.HBM)
    slabs = pl.pallas_call(
        slab_kernel,
        out_shape=tuple(jax.ShapeDtypeStruct((n * size, channels), BF16) for n in (1, 1, 2)),
        in_specs=[SMEM_SPEC, hbm],
        out_specs=(VMEM_SPEC,) * 3,
        scratch_shapes=[pltpu.SemaphoreType.DMA((3,))],
        name="slabs",
    )(
        jnp.stack([offset(corner, core, 0), offset(corner, core, 1), offset(corner ^ 3, core, 0)]),
        in_hbm(harmonic_table),
    )

    own = orbitals[0]
    weight = ang_weight[None, :]
    degree = channel_degree(channel_lm)[None, :]
    cont = continuum.reshape(NC * points, channels)
    place = jnp.stack([x, offset(corner, core, 1)]).astype(jnp.int32)
    part_shape = jax.ShapeDtypeStruct((NC * half, channels), BF16)
    phi_shape = jax.ShapeDtypeStruct((half, quad), BF16)

    other = over_x(own)
    first_a = over_x(slabs[0])
    first_b = over_x(slabs[1])
    last = over_x(slabs[2])
    part, phi, psi, own_ends, table = pl.pallas_call(
        functools.partial(own_kernel, step),
        out_shape=(
            part_shape,
            phi_shape,
            jax.ShapeDtypeStruct((NC * points, quad), BF16),
            jax.ShapeDtypeStruct((4 * NC, channels), F32),
            jax.ShapeDtypeStruct((quad, channels), BF16),
        ),
        in_specs=[SMEM_SPEC] + [VMEM_SPEC] * 4 + [pl.BlockSpec(memory_space=pltpu.HBM)],
        out_specs=(ANY_SPEC,) * 2 + (VMEM_SPEC,) * 3,
        scratch_shapes=[
            pltpu.VMEM((NC * half, channels), BF16),
            pltpu.VMEM((half, quad), BF16),
            pltpu.VMEM(((1 + NC) * points, channels), BF16),
            pltpu.VMEM((NC * points, quad), BF16),
            pltpu.VMEM((NC * points, TILE), F32),
            pltpu.SemaphoreType.DMA((quad // CHUNK,)),
        ],
        compiler_params=pltpu.CompilerParams(vmem_limit_bytes=16 << 20),
        name="own_orbital",
    )(place, own, cont, weight, degree, in_hbm(after(harmonic_table, slabs[0])))
    other_part, other_phi, ends = pl.pallas_call(
        functools.partial(other_kernel, step),
        out_shape=(
            part_shape,
            phi_shape,
            jax.ShapeDtypeStruct((4 * NP, channels), F32),
        ),
        in_specs=[SMEM_SPEC] + [VMEM_SPEC] * 6,
        out_specs=(ANY_SPEC, ANY_SPEC, VMEM_SPEC),
        scratch_shapes=[
            pltpu.VMEM((NC * half, channels), BF16),
            pltpu.VMEM((half, quad), BF16),
            pltpu.VMEM((NC * points, quad), BF16),
            pltpu.VMEM((NC * points, TILE), F32),
            pltpu.SemaphoreType.DMA((3,)),
        ],
        compiler_params=pltpu.CompilerParams(vmem_limit_bytes=8 << 20),
        name="other_orbital",
    )(place, other, psi, weight, degree, own_ends, table)
    ends = ends.reshape(4, NP, channels)
    ahead_rate = (degree + 1.0) * step
    behind_rate = degree * step

    def ahead_by(count):
        return jnp.exp(-ahead_rate * count)

    def behind_by(count):
        return jnp.exp(-behind_rate * count)

    low_end, high_end, low_start, high_start = ends[0], ends[1], ends[2], ends[3]
    block_end = high_end + ahead_by(half) * low_end
    block_start = low_start + behind_by(half) * high_start
    u = g % 4
    both = jnp.concatenate([block_end, block_start], axis=0)
    message = both.astype(BF16)
    first_a = after(first_a, message)
    by_y_a, by_z_a = flip(first_a, 2), flip(first_a, 4)
    earlier = jnp.zeros((NP, channels), F32)
    later = jnp.zeros((NP, channels), F32)
    row_end = ahead_by(points * (3 - u)) * block_end
    row_start = behind_by(points * u) * block_start
    for bits in (1, 2, 3):
        came = flip(message, bits).astype(F32)
        v = u ^ bits
        distance = jnp.abs(u - v) - 1
        before = v < u
        earlier += jnp.where(before, ahead_by(points * distance), 0.0) * came[:NP]
        later += jnp.where(before, 0.0, behind_by(points * distance)) * came[NP:]
        row_end += ahead_by(points * (3 - v)) * came[:NP]
        row_start += behind_by(points * v) * came[NP:]
    row_end = after(row_end.astype(BF16), first_a, first_b)
    row_start = after(row_start.astype(BF16), first_a, first_b)
    for shift in (1, 2, 3):
        message = jnp.where(z + shift < 4, row_end, row_start)
        came = lax.ppermute(message, "grid", [(n, (n + 4 * shift) % 16) for n in everyone])
        came = after(came, by_y_a, by_z_a, last)
        came = came.astype(F32)
        source = (z - shift) % 4
        before = source < z
        distance = jnp.abs(z - source) - 1
        earlier += jnp.where(before, ahead_by(points * (4 * distance + u)), 0.0) * came
        later += jnp.where(before, 0.0, behind_by(points * (4 * distance + 3 - u))) * came
    upper_earlier = low_end + ahead_by(half) * earlier
    lower_later = high_start + behind_by(half) * later
    theirs = jnp.concatenate(
        [jnp.where(x == 0, upper_earlier, earlier), jnp.where(x == 0, later, lower_later)], axis=0
    )
    terms, rest = [], weight
    for _ in range(3):
        terms.append(lax.reduce_precision(rest, 8, 7))
        rest = rest - terms[-1]
    terms = jnp.pad(jnp.concatenate(terms, axis=0), ((0, NP - 3), (0, channels - quad)))
    theirs = jnp.concatenate([theirs, terms], axis=0)
    theirs = theirs.astype(BF16)
    arrived = over_x(theirs)
    earlier = jnp.where(x == 0, earlier, upper_earlier)
    later = jnp.where(x == 0, lower_later, later)
    first_b = after(first_b, row_end)
    received = [first_a, first_b, last]
    received += [by_y_a, by_z_a, flip(first_b, 2), flip(first_b, 4)]
    which = [(corner, 0), (corner, 1), (corner ^ 3, 0)]
    which += [(corner ^ 1, 0), (corner ^ 2, 0), (corner ^ 1, 1), (corner ^ 2, 1)]
    far = received + [flip(value, 1) for value in received]
    far[4:6] = [in_hbm(value) for value in far[4:6]]
    offsets = [offset(w, core, n) for w, n in which] + [offset(w, 1 - core, n) for w, n in which]
    places = jnp.stack([x] + offsets).astype(jnp.int32)

    send, keep = pl.pallas_call(
        functools.partial(finish_kernel, step, pieces),
        out_shape=(
            jax.ShapeDtypeStruct((NC * half, channels // 2), BF16),
            jax.ShapeDtypeStruct((NC * half, channels // 2), F32),
        ),
        in_specs=[SMEM_SPEC, hbm, VMEM_SPEC, hbm] + [VMEM_SPEC] * 5 + [hbm] * 5 + [ANY_SPEC] * pieces,
        out_specs=(ANY_SPEC,) * 2,
        scratch_shapes=[
            pltpu.VMEM((1, quad), F32),
            pltpu.VMEM((NC * half, channels // 2), BF16),
            pltpu.VMEM((NC * half, channels // 2), F32),
            pltpu.VMEM((NP * half, channels), BF16),
            pltpu.VMEM((quad, channels), BF16),
            pltpu.VMEM((quad, channels), BF16),
            pltpu.VMEM(((NI + NC) * half, channels), BF16),
            pltpu.VMEM((NP * half, quad), BF16),
            pltpu.VMEM((NP * half, quad), BF16),
            pltpu.VMEM((NI * half, 2 * quad), BF16),
            pltpu.VMEM((NP * half, channels), BF16),
            pltpu.VMEM((NC * half, 2 * quad), BF16),
            pltpu.VMEM((half, NP, TILE), F32),
            pltpu.VMEM((half, NP, TILE), F32),
            pltpu.SemaphoreType.DMA((pieces + 6 + NC,)),
        ],
        compiler_params=pltpu.CompilerParams(vmem_limit_bytes=30 << 20),
        name="finish",
    )(
        places, in_hbm(own), other, in_hbm(cont), weight, degree, earlier, later, arrived,
        in_hbm(part), in_hbm(other_part), in_hbm(phi), in_hbm(other_phi), in_hbm(harmonic_table), *far,
    )
    came = over_x(send)
    out = pl.pallas_call(
        place_kernel,
        out_shape=jax.ShapeDtypeStruct((NC, points, channels // 2), F32),
        in_specs=[SMEM_SPEC, VMEM_SPEC, VMEM_SPEC],
        out_specs=VMEM_SPEC,
        name="place",
    )(place, keep, came)
    return jnp.transpose(out, (2, 0, 1))


def solution(mesh):
    small = dict(mesh.shape) == {"orb": 2, "grid": 16}
    return jax.shard_map(
        shards_by_table if small else shards,
        mesh=mesh,
        in_specs=(P("orb", "grid", None), P(None, "grid", None), P("orb", None), P("orb"), P()),
        out_specs=P("orb", None, "grid"),
        check_vma=False,
    )
```

```python
import functools
import math

import jax
import jax.numpy as jnp
from jax import lax
from jax.experimental import pallas as pl
from jax.experimental.pallas import tpu as pltpu
from jax.sharding import PartitionSpec as P

LMAX = 47
LM = 2304


LOG_SPAN = 7.0


def combine(earlier, later):
    return (earlier[0] * later[0], earlier[1] * later[0] + later[1])


def channel_degree(lm_index):
    levels = jnp.arange(1, LMAX + 1, dtype=jnp.int32)
    return jnp.sum((lm_index[:, None] >= levels * levels).astype(jnp.float32), axis=1)


def line_sums(forward_source, backward_source, decay_rate, block_size):
    lead_first, lead_second, count, channels = forward_source.shape
    block_count = count // block_size
    forward_blocks = forward_source.reshape(
        lead_first, lead_second, block_count, block_size, channels
    )
    backward_blocks = backward_source.reshape(
        lead_first, lead_second, block_count, block_size, channels
    )
    forward = forward_blocks
    backward = backward_blocks
    for distance in range(1, block_size):
        factor = jnp.exp(-decay_rate * distance)
        padding = jnp.zeros((lead_first, lead_second, block_count, distance, channels), jnp.float32)
        forward = forward + factor * jnp.concatenate(
            [padding, forward_blocks[:, :, :, : block_size - distance]], axis=3
        )
        backward = backward + factor * jnp.concatenate(
            [backward_blocks[:, :, :, distance:], padding], axis=3
        )
    block_decay = jnp.broadcast_to(
        jnp.exp(-decay_rate * block_size), (lead_first, lead_second, block_count, channels)
    )
    forward_total = lax.associative_scan(
        combine, (block_decay, forward[:, :, :, block_size - 1]), axis=2
    )[1]
    backward_total = lax.associative_scan(
        combine, (block_decay, backward[:, :, :, 0]), reverse=True, axis=2
    )[1]
    boundary = jnp.zeros((lead_first, lead_second, 1, channels), jnp.float32)
    earlier_sum = jnp.concatenate([boundary, forward_total[:, :, : block_count - 1]], axis=2)
    later_sum = jnp.concatenate([backward_total[:, :, 1:], boundary], axis=2)
    offsets = jnp.arange(block_size, dtype=jnp.float32)[:, None]
    forward = forward + jnp.exp(-decay_rate * (offsets + 1.0)) * earlier_sum[:, :, :, None, :]
    backward = (
        backward + jnp.exp(-decay_rate * (block_size - offsets)) * later_sum[:, :, :, None, :]
    )
    shape = forward_source.shape
    return (
        forward.reshape(shape),
        backward.reshape(shape),
        forward_total[:, :, block_count - 1],
        backward_total[:, :, 0],
    )


def local_lines(density, degree, points):
    count = density.shape[2]
    increment = LOG_SPAN / points
    positions = jnp.arange(count, dtype=jnp.int32).astype(jnp.float32)[:, None]
    radius = jnp.exp((positions + 1.0 - points) * increment)
    decay_rate = degree * increment
    source = increment * radius * density
    scaled = increment * density
    forward, backward, forward_end, backward_end = line_sums(
        source, scaled, decay_rate, math.gcd(count, 16)
    )
    return (forward, backward, forward_end, backward_end, radius, scaled, decay_rate)


def finish_potential(forward, backward, radius, scaled, degree):
    factor = 4.0 / (2.0 * degree + 1.0)
    return factor * (forward / radius + backward - scaled)


def shards(orbitals, continuum, harmonic_table, ang_weight, channel_lm):
    analysis = (ang_weight[:, None] * harmonic_table.astype(jnp.float32)).astype(jnp.bfloat16)
    phi_ang = jnp.einsum(
        "al,irl->ira",
        harmonic_table,
        lax.all_gather(orbitals, "orb", axis=0, tiled=True),
        preferred_element_type=jnp.float32,
    ).astype(jnp.bfloat16)
    continuum_angular = jnp.einsum(
        "al,krl->kra", harmonic_table, continuum, preferred_element_type=jnp.float32
    ).astype(jnp.bfloat16)
    pair_values = (
        phi_ang.astype(jnp.float32)[:, None] * continuum_angular.astype(jnp.float32)[None]
    ).astype(jnp.bfloat16)
    density = lax.psum_scatter(
        jnp.einsum(
            "al,ikra->ikrl", analysis, pair_values, preferred_element_type=jnp.float32
        ).astype(jnp.bfloat16),
        "orb",
        scatter_dimension=0,
        tiled=True,
    )
    local_count = LM // lax.axis_size("grid")
    local_channel_index = lax.dynamic_slice_in_dim(
        channel_lm, lax.axis_index("grid") * local_count, local_count
    )
    degree = channel_degree(local_channel_index)
    line_density = lax.all_to_all(density, "grid", split_axis=3, concat_axis=2, tiled=True)
    points = line_density.shape[2]
    forward, backward, forward_end, backward_end, radius, scaled, decay_rate = local_lines(
        line_density.astype(jnp.float32), degree, points
    )
    potential = finish_potential(forward, backward, radius, scaled, degree).astype(jnp.bfloat16)
    radial_potential = lax.all_to_all(potential, "grid", split_axis=2, concat_axis=3, tiled=True)
    pot_ang = jnp.einsum(
        "al,ikrl->ikra",
        harmonic_table,
        lax.all_gather(radial_potential, "orb", axis=0, tiled=True),
        preferred_element_type=jnp.float32,
    )
    weighted_values = jnp.sum(phi_ang.astype(jnp.float32)[:, None] * pot_ang, axis=0)
    product = weighted_values.astype(jnp.bfloat16)
    return -lax.psum_scatter(
        jnp.einsum("al,kra->lkr", analysis, product, preferred_element_type=jnp.float32),
        "orb",
        scatter_dimension=0,
        tiled=True,
    )


NC = 4
NI = 2
NP = NI * NC
CHUNK = 256
WIDE = 1280
TILE = 768
F32 = jnp.float32
BF16 = jnp.bfloat16


def dot_nt(a, b):
    return lax.dot_general(a, b, (((1,), (1,)), ((), ())), preferred_element_type=F32)


def dot_nn(a, b):
    return jnp.dot(a, b, preferred_element_type=F32)


def span_of(index, size):
    return pl.ds(pl.multiple_of(index * size, size), size)


def store_pairs(values, weight, points, pairs, span):
    phi = values[: NI * points].astype(F32) * weight
    psi = values[NI * points :].astype(F32)
    for i in range(NI):
        for k in range(NC):
            product = phi[i * points : (i + 1) * points] * psi[k * points : (k + 1) * points]
            row = (i * NC + k) * points
            pairs[row : row + points, span] = product.astype(BF16)


def angular_density(step, x, values_of, store, table, weight, degree_ref, part_ref, ends_at, pairs, work):
    half = part_ref.shape[0] // NC
    points = 2 * half
    steps = table.shape[0] // CHUNK

    def angular(i, carry):
        span = span_of(i, CHUNK)
        phi, psi = values_of(i, span)
        low_high = phi.reshape(2, half, CHUNK)
        store(span, jnp.where(x == 0, low_high[0], low_high[1]), psi)
        phi = phi.astype(F32) * weight[:, span]
        psi = psi.astype(F32)
        for k in range(NC):
            rows = slice(k * points, (k + 1) * points)
            pairs[rows, span] = (phi * psi[rows]).astype(BF16)
        return carry

    lax.fori_loop(0, steps, angular, 0)

    def density(t, carry):
        span = span_of(t, TILE)
        degree = degree_ref[:, span]
        work[...] = dot_nn(pairs[...], table[:, span])
        position = lax.broadcasted_iota(jnp.int32, (half, TILE), 0).astype(F32)
        ahead = jnp.exp((degree + 1.0) * step * (position - (half - 1.0)))
        behind = jnp.exp(-degree * step * position)
        for k in range(NC):
            low = work[k * points : k * points + half, :]
            high = work[k * points + half : (k + 1) * points, :]
            part_ref[k * half : (k + 1) * half, span] = jnp.where(x == 0, low, high).astype(BF16)
            ends = (low * ahead, high * ahead, low * behind, high * behind)
            for n in range(4):
                ends_at(n, k, span, jnp.sum(ends[n], axis=0, keepdims=True))
        return carry

    lax.fori_loop(0, table.shape[1] // TILE, density, 0)


def own_kernel(
    step, place, own, cont, weight, degree_ref, table_hbm,
    part_any, phi_any, psi_ref, ends_ref, table,
    part_ref, phi_ref, rows, pairs, work, sems,
):
    points = own.shape[0]
    steps = table.shape[0] // CHUNK

    def fetch(i):
        return pltpu.make_async_copy(
            table_hbm.at[span_of(i, CHUNK)], table.at[span_of(i, CHUNK)], sems.at[i]
        )

    for i in range(steps):
        fetch(i).start()
    rows[:points, :] = own[...]
    rows[points:, :] = cont[...]

    def values_of(i, span):
        fetch(i).wait()
        values = dot_nt(rows[...], table[span, :]).astype(BF16)
        return values[:points], values[points:]

    def store(span, phi, psi):
        phi_ref[:, span] = phi
        psi_ref[:, span] = psi

    def ends_at(n, k, span, value):
        ends_ref[n * NC + k : n * NC + k + 1, span] = value

    angular_density(
        step, place[0], values_of, store, table, weight, degree_ref, part_ref, ends_at, pairs, work
    )
    copies = [
        pltpu.make_async_copy(part_ref, part_any, sems.at[0]),
        pltpu.make_async_copy(phi_ref, phi_any, sems.at[1]),
    ]
    for copy in copies:
        copy.start()
    for copy in copies:
        copy.wait()


def other_kernel(
    step, place, other, psi_ref, weight, degree_ref, own_ends, table,
    part_any, phi_any, ends_ref,
    part_ref, phi_ref, pairs, work, sems,
):
    x = place[0]

    def values_of(i, span):
        return dot_nt(other[...], table[span, :]).astype(BF16), psi_ref[:, span]

    def store(span, phi, psi):
        phi_ref[:, span] = phi

    def ends_at(n, k, span, value):
        ends_ref[pl.ds(n * NP + (1 - x) * NC + k, 1), span] = value

    for n in range(4):
        for k in range(NC):
            ends_ref[pl.ds(n * NP + x * NC + k, 1), :] = own_ends[n * NC + k : n * NC + k + 1, :]
    angular_density(
        step, x, values_of, store, table, weight, degree_ref, part_ref, ends_at, pairs, work
    )
    copies = [
        pltpu.make_async_copy(part_ref, part_any, sems.at[0]),
        pltpu.make_async_copy(phi_ref, phi_any, sems.at[1]),
    ]
    for copy in copies:
        copy.start()
    for copy in copies:
        copy.wait()


def finish_kernel(
    step, pieces, place, own, other, cont, weight, degree_ref, earlier, later, arrived,
    part_any, other_part_any, phi_any, other_phi_any, table_hbm, *refs
):
    far_hbm = refs[:pieces]
    send_any, keep_any, far_weight, send_ref, keep_ref, part, table, far_table, rows, pairs, sorted_pairs, phi_all, pot, product, work, total, sems = refs[pieces:]
    x = place[0]
    points = own.shape[0]
    half = points // 2
    quad, channels = table.shape
    steps = quad // WIDE

    def fetch_far(n):
        size = far_hbm[n].shape[0]
        start = pl.multiple_of(place[1 + n], quad // 16)
        return pltpu.make_async_copy(far_hbm[n], far_table.at[pl.ds(start, size)], sems.at[n])

    def fetch_rows():
        near = span_of(x, half)
        yield pltpu.make_async_copy(own.at[near], rows.at[near], sems.at[pieces])
        for k in range(NC):
            at = span_of(2 * k + x, half)
            to = pl.ds((NI + k) * half, half)
            yield pltpu.make_async_copy(cont.at[at], rows.at[to], sems.at[pieces + 1 + k])

    fetch_table = pltpu.make_async_copy(table_hbm, table, sems.at[pieces + 1 + NC])
    for copy in fetch_rows():
        copy.start()

    for n in range(pieces):
        fetch_far(n).start()
    near = [
        pltpu.make_async_copy(phi_any, phi_all.at[span_of(x, half), pl.ds(0, quad)], sems.at[pieces + 2 + NC]),
        pltpu.make_async_copy(other_phi_any, phi_all.at[span_of(1 - x, half), pl.ds(0, quad)], sems.at[pieces + 3 + NC]),
        pltpu.make_async_copy(part_any, part.at[span_of(x, NC * half)], sems.at[pieces + 4 + NC]),
        pltpu.make_async_copy(other_part_any, part.at[span_of(1 - x, NC * half)], sems.at[pieces + 5 + NC]),
    ]
    for copy in near:
        copy.start()
    fetch_table.start()
    rows[span_of(1 - x, half), :] = other[span_of(x, half), :]
    far_weight[...] = jnp.zeros_like(far_weight)
    for row in (2 * NP + 2, 2 * NP + 1, 2 * NP):
        far_weight[...] += arrived[row : row + 1, :quad].astype(F32)
    for copy in fetch_rows():
        copy.wait()
    for n in range(pieces):
        fetch_far(n).wait()

    shape = (NP * half, NP * half)
    row, column = (lax.broadcasted_iota(jnp.int32, shape, n) for n in range(2))
    by_point = ((row & (NP - 1)) * half + (row >> 3) == column).astype(F32).astype(BF16)
    by_pair = ((column & (NP - 1)) * half + (column >> 3) == row).astype(F32).astype(BF16)

    def angular(i, carry):
        span = span_of(i, WIDE)
        values = dot_nt(rows[...], far_table[span, :]).astype(BF16)
        store_pairs(values, far_weight[:, span], half, pairs, span)
        phi_all[:, span_of(i + steps, WIDE)] = values[: NI * half]
        sorted_pairs[:, span] = dot_nn(by_point, pairs[:, span]).astype(BF16)
        return carry

    lax.fori_loop(0, steps, angular, 0)
    for copy in near:
        copy.wait()

    def radial(t, carry):
        span = span_of(t, TILE)
        degree = degree_ref[:, span]
        shrink_ahead = jnp.exp(-(degree + 1.0) * step)
        shrink_behind = jnp.exp(-degree * step)
        factor = 4.0 * step / (2.0 * degree + 1.0)
        density = dot_nn(sorted_pairs[...], far_table[:, span]) + dot_nn(by_point, part[:, span])
        work[...] = density.reshape(half, NP, TILE)
        came = arrived[:, span].astype(F32)
        ahead = earlier[:, span] + came[:NP]
        behind = (later[:, span] + came[NP : 2 * NP]) * shrink_behind
        for j in range(half):
            ahead = ahead * shrink_ahead + work[j]
            total[j] = ahead
        for j in range(half - 1, -1, -1):
            total[j] = factor * (total[j] + behind)
            behind = (behind + work[j]) * shrink_behind
        potential = total[...].reshape(NP * half, TILE).astype(BF16)
        pot[:, span] = dot_nn(by_pair, potential).astype(BF16)
        return carry

    lax.fori_loop(0, channels // TILE, radial, 0)

    def weigh(source, weight_at, first):
        def chunk(i, carry):
            span = span_of(i, WIDE)
            at = span_of(i + first, WIDE)
            angle = dot_nt(pot[...], source[span, :])
            values = phi_all[:, at].astype(F32) * weight_at[:, span]
            for k in range(NC):
                value = jnp.zeros((half, WIDE), F32)
                for o in range(NI):
                    row = (o * NC + k) * half
                    value += values[o * half : (o + 1) * half] * angle[row : row + half]
                product[k * half : (k + 1) * half, at] = value.astype(BF16)
            return carry

        lax.fori_loop(0, steps, chunk, 0)

    weigh(far_table, far_weight, steps)
    fetch_table.wait()
    weigh(table, weight, 0)
    share = channels // 2
    leave = []
    for n, (out, to, first) in enumerate(
        ((send_ref, send_any, (1 - x) * share), (keep_ref, keep_any, x * share))
    ):
        at = pl.ds(pl.multiple_of(first, share), share)
        value = dot_nn(product[:, :quad], table[:, at]) + dot_nn(product[:, quad:], far_table[:, at])
        out[...] = (-value).astype(out.dtype)
        leave.append(pltpu.make_async_copy(out, to, sems.at[n]))
        leave[n].start()
    for copy in leave:
        copy.wait()


def slab_kernel(place, table, *refs):
    sems = refs[-1]
    copies = []
    for n, out in enumerate(refs[:-1]):
        start = pl.multiple_of(place[n], 80)
        copies.append(pltpu.make_async_copy(table.at[pl.ds(start, out.shape[0])], out, sems.at[n]))
    for copy in copies:
        copy.start()
    for copy in copies:
        copy.wait()


def place_kernel(place, keep, came, out_ref):
    x = place[0]
    half = keep.shape[0] // NC
    out_ref[:, span_of(x, half), :] = keep[...].reshape(NC, half, -1)
    out_ref[:, span_of(1 - x, half), :] = came[...].astype(F32).reshape(NC, half, -1)


VMEM_SPEC = pl.BlockSpec(memory_space=pltpu.VMEM)
SMEM_SPEC = pl.BlockSpec(memory_space=pltpu.SMEM)
HBM_SPEC = pl.BlockSpec(memory_space=pl.ANY)
ANY_SPEC = HBM_SPEC


def shards_by_table(orbitals, continuum, harmonic_table, ang_weight, channel_lm):
    quad, channels = harmonic_table.shape
    points = orbitals.shape[1]
    half = points // 2
    step = LOG_SPAN / (points * lax.axis_size("grid"))
    x = lax.axis_index("orb")
    g = lax.axis_index("grid")
    core, y, z = g % 2, (g // 2) % 2, g // 4
    across = [(0, 1), (1, 0)]
    everyone = range(16)

    def over_x(value):
        return lax.ppermute(value, "orb", across)

    def flip(value, bits):
        return lax.ppermute(value, "grid", [(n, n ^ bits) for n in everyone])

    pieces = 14
    size = quad // 16
    corner = 2 * (z % 2) + y

    def offset(which, side, n):
        return ((which * 2 + side) * 2 + n) * size

    def after(value, *others):
        return lax.optimization_barrier((value, *others))[0]

    def in_hbm(value):
        return pltpu.with_memory_space_constraint(value, pltpu.HBM)

    hbm = pl.BlockSpec(memory_space=pltpu.HBM)
    slabs = pl.pallas_call(
        slab_kernel,
        out_shape=tuple(jax.ShapeDtypeStruct((n * size, channels), BF16) for n in (1, 1, 2)),
        in_specs=[SMEM_SPEC, hbm],
        out_specs=(VMEM_SPEC,) * 3,
        scratch_shapes=[pltpu.SemaphoreType.DMA((3,))],
        name="slabs",
    )(
        jnp.stack([offset(corner, core, 0), offset(corner, core, 1), offset(corner ^ 3, core, 0)]),
        in_hbm(harmonic_table),
    )

    own = orbitals[0]
    weight = ang_weight[None, :]
    degree = channel_degree(channel_lm)[None, :]
    cont = continuum.reshape(NC * points, channels)
    place = jnp.stack([x, offset(corner, core, 1)]).astype(jnp.int32)
    part_shape = jax.ShapeDtypeStruct((NC * half, channels), BF16)
    phi_shape = jax.ShapeDtypeStruct((half, quad), BF16)

    other = over_x(own)
    first_a = over_x(slabs[0])
    first_b = over_x(slabs[1])
    last = over_x(slabs[2])
    part, phi, psi, own_ends, table = pl.pallas_call(
        functools.partial(own_kernel, step),
        out_shape=(
            part_shape,
            phi_shape,
            jax.ShapeDtypeStruct((NC * points, quad), BF16),
            jax.ShapeDtypeStruct((4 * NC, channels), F32),
            jax.ShapeDtypeStruct((quad, channels), BF16),
        ),
        in_specs=[SMEM_SPEC] + [VMEM_SPEC] * 4 + [pl.BlockSpec(memory_space=pltpu.HBM)],
        out_specs=(ANY_SPEC,) * 2 + (VMEM_SPEC,) * 3,
        scratch_shapes=[
            pltpu.VMEM((NC * half, channels), BF16),
            pltpu.VMEM((half, quad), BF16),
            pltpu.VMEM(((1 + NC) * points, channels), BF16),
            pltpu.VMEM((NC * points, quad), BF16),
            pltpu.VMEM((NC * points, TILE), F32),
            pltpu.SemaphoreType.DMA((quad // CHUNK,)),
        ],
        compiler_params=pltpu.CompilerParams(vmem_limit_bytes=16 << 20),
        name="own_orbital",
    )(place, own, cont, weight, degree, in_hbm(after(harmonic_table, slabs[0])))
    other_part, other_phi, ends = pl.pallas_call(
        functools.partial(other_kernel, step),
        out_shape=(
            part_shape,
            phi_shape,
            jax.ShapeDtypeStruct((4 * NP, channels), F32),
        ),
        in_specs=[SMEM_SPEC] + [VMEM_SPEC] * 6,
        out_specs=(ANY_SPEC, ANY_SPEC, VMEM_SPEC),
        scratch_shapes=[
            pltpu.VMEM((NC * half, channels), BF16),
            pltpu.VMEM((half, quad), BF16),
            pltpu.VMEM((NC * points, quad), BF16),
            pltpu.VMEM((NC * points, TILE), F32),
            pltpu.SemaphoreType.DMA((3,)),
        ],
        compiler_params=pltpu.CompilerParams(vmem_limit_bytes=8 << 20),
        name="other_orbital",
    )(place, other, psi, weight, degree, own_ends, table)
    ends = ends.reshape(4, NP, channels)
    ahead_rate = (degree + 1.0) * step
    behind_rate = degree * step

    def ahead_by(count):
        return jnp.exp(-ahead_rate * count)

    def behind_by(count):
        return jnp.exp(-behind_rate * count)

    low_end, high_end, low_start, high_start = ends[0], ends[1], ends[2], ends[3]
    block_end = high_end + ahead_by(half) * low_end
    block_start = low_start + behind_by(half) * high_start
    u = g % 4
    both = jnp.concatenate([block_end, block_start], axis=0)
    message = both.astype(BF16)
    first_a = after(first_a, message)
    by_y_a, by_z_a = flip(first_a, 2), flip(first_a, 4)
    earlier = jnp.zeros((NP, channels), F32)
    later = jnp.zeros((NP, channels), F32)
    row_end = ahead_by(points * (3 - u)) * block_end
    row_start = behind_by(points * u) * block_start
    for bits in (1, 2, 3):
        came = flip(message, bits).astype(F32)
        v = u ^ bits
        distance = jnp.abs(u - v) - 1
        before = v < u
        earlier += jnp.where(before, ahead_by(points * distance), 0.0) * came[:NP]
        later += jnp.where(before, 0.0, behind_by(points * distance)) * came[NP:]
        row_end += ahead_by(points * (3 - v)) * came[:NP]
        row_start += behind_by(points * v) * came[NP:]
    row_end = after(row_end.astype(BF16), first_a, first_b)
    row_start = after(row_start.astype(BF16), first_a, first_b)
    for shift in (1, 2, 3):
        message = jnp.where(z + shift < 4, row_end, row_start)
        came = lax.ppermute(message, "grid", [(n, (n + 4 * shift) % 16) for n in everyone])
        came = after(came, by_y_a, by_z_a, last)
        came = came.astype(F32)
        source = (z - shift) % 4
        before = source < z
        distance = jnp.abs(z - source) - 1
        earlier += jnp.where(before, ahead_by(points * (4 * distance + u)), 0.0) * came
        later += jnp.where(before, 0.0, behind_by(points * (4 * distance + 3 - u))) * came
    upper_earlier = low_end + ahead_by(half) * earlier
    lower_later = high_start + behind_by(half) * later
    theirs = jnp.concatenate(
        [jnp.where(x == 0, upper_earlier, earlier), jnp.where(x == 0, later, lower_later)], axis=0
    )
    terms, rest = [], weight
    for _ in range(3):
        terms.append(lax.reduce_precision(rest, 8, 7))
        rest = rest - terms[-1]
    terms = jnp.pad(jnp.concatenate(terms, axis=0), ((0, NP - 3), (0, channels - quad)))
    theirs = jnp.concatenate([theirs, terms], axis=0)
    theirs = theirs.astype(BF16)
    arrived = over_x(theirs)
    earlier = jnp.where(x == 0, earlier, upper_earlier)
    later = jnp.where(x == 0, lower_later, later)
    first_b = after(first_b, row_end)
    received = [first_a, first_b, last]
    received += [by_y_a, by_z_a, flip(first_b, 2), flip(first_b, 4)]
    which = [(corner, 0), (corner, 1), (corner ^ 3, 0)]
    which += [(corner ^ 1, 0), (corner ^ 2, 0), (corner ^ 1, 1), (corner ^ 2, 1)]
    far = received + [flip(value, 1) for value in received]
    far[4:6] = [in_hbm(value) for value in far[4:6]]
    offsets = [offset(w, core, n) for w, n in which] + [offset(w, 1 - core, n) for w, n in which]
    places = jnp.stack([x] + offsets).astype(jnp.int32)

    send, keep = pl.pallas_call(
        functools.partial(finish_kernel, step, pieces),
        out_shape=(
            jax.ShapeDtypeStruct((NC * half, channels // 2), BF16),
            jax.ShapeDtypeStruct((NC * half, channels // 2), F32),
        ),
        in_specs=[SMEM_SPEC, hbm, VMEM_SPEC, hbm] + [VMEM_SPEC] * 5 + [hbm] * 5 + [ANY_SPEC] * pieces,
        out_specs=(ANY_SPEC,) * 2,
        scratch_shapes=[
            pltpu.VMEM((1, quad), F32),
            pltpu.VMEM((NC * half, channels // 2), BF16),
            pltpu.VMEM((NC * half, channels // 2), F32),
            pltpu.VMEM((NP * half, channels), BF16),
            pltpu.VMEM((quad, channels), BF16),
            pltpu.VMEM((quad, channels), BF16),
            pltpu.VMEM(((NI + NC) * half, channels), BF16),
            pltpu.VMEM((NP * half, quad), BF16),
            pltpu.VMEM((NP * half, quad), BF16),
            pltpu.VMEM((NI * half, 2 * quad), BF16),
            pltpu.VMEM((NP * half, channels), BF16),
            pltpu.VMEM((NC * half, 2 * quad), BF16),
            pltpu.VMEM((half, NP, TILE), F32),
            pltpu.VMEM((half, NP, TILE), F32),
            pltpu.SemaphoreType.DMA((pieces + 6 + NC,)),
        ],
        compiler_params=pltpu.CompilerParams(vmem_limit_bytes=30 << 20),
        name="finish",
    )(
        places, in_hbm(own), other, in_hbm(cont), weight, degree, earlier, later, arrived,
        in_hbm(part), in_hbm(other_part), in_hbm(phi), in_hbm(other_phi), in_hbm(harmonic_table), *far,
    )
    came = over_x(send)
    out = pl.pallas_call(
        place_kernel,
        out_shape=jax.ShapeDtypeStruct((NC, points, channels // 2), F32),
        in_specs=[SMEM_SPEC, VMEM_SPEC, VMEM_SPEC],
        out_specs=VMEM_SPEC,
        name="place",
    )(place, keep, came)
    return jnp.transpose(out, (2, 0, 1))


def solution(mesh):
    small = dict(mesh.shape) == {"orb": 2, "grid": 16}
    return jax.shard_map(
        shards_by_table if small else shards,
        mesh=mesh,
        in_specs=(P("orb", "grid", None), P(None, "grid", None), P("orb", None), P("orb"), P()),
        out_specs=P("orb", None, "grid"),
        check_vma=False,
    )
```
